256 devices in a mesh: rows: 32 (over y, z), samples: 8 (over x, core).
Axes of the slice: x: 4, y: 4, z: 8, core: 2. Of those that a mesh axis runs over, the one named last changes fastest.
Arguments:
- matrix_block: bfloat16 [32768, 20480], P('rows', 'samples'), may hold values from -6 to 6
- sketch_matrix: bfloat16 [20480, 384], P('samples'), may hold values from -0.0390625 to 0.0390625
- local_pivots: int32 [32, 3, 256], P('rows'), may hold values from 0 to 511, as said below
- upper_pivots: int32 [30, 256], replicated, may hold values from 0 to 511, as said below
Outputs:
- leaf_basis: float32 [32768, 384], P(('rows', 'samples'))
- device_basis: float32 [16384, 384], P('rows')
- inner_basis: float32 [16384, 384], P('rows')
The draws below stay inside these ranges and needn't reach their ends.
Inputs may be any that keep to these rules, and one draw needn't show every extreme that they name: `local_pivots`: each row holds 256 distinct indices. `upper_pivots`: each row holds 256 distinct indices.
All inputs are finite; a program needn't handle non-finite values.
Results may differ from the reference program's by a relative error of at most 0.0003.
Values sent between devices are 32-bit elements; how exact they have to be, the bound alone decides.
A program may use at most 128 MiB of HBM per device.

```python
import math
import jax
import jax.numpy as jnp
from jax import lax

LEAF = 512
RANK = 256
SKETCH = 384
CLUSTERS = 32
ROWS = 32768
COLS = 20480


def pivot_rows(key, row_count):
    keys = jax.random.split(key, row_count)

    def one_row(one_key):
        return jax.random.permutation(one_key, LEAF)[:RANK]
    return jax.vmap(one_row)(keys).astype(jnp.int32)


def draw_local_pivots(key, part):
    return pivot_rows(jax.random.fold_in(key, 11), CLUSTERS * 3).reshape(CLUSTERS, 3, RANK)


def draw_upper_pivots(key, part):
    return pivot_rows(jax.random.fold_in(key, 23), CLUSTERS - 2)


def level_of(rng, dims, pieces, low, top_value):
    def one(dim, blocks):
        steps = jax.random.uniform(jax.random.fold_in(jax.random.fold_in(rng, 6), dim), (blocks,), jnp.float32, low / len(pieces), top_value / len(pieces))
        return jnp.repeat(jnp.exp(steps), dims[dim] // blocks).reshape((-1,) + (1,) * (len(dims) - dim - 1))

    factor_of = one(*pieces[0])
    for cut in pieces[1:]:
        factor_of = factor_of * one(*cut)
    return factor_of


def noise(own_key, shape, deviation, reach, pieces=(), held_as=jnp.bfloat16):
    entries = deviation * jax.random.normal(own_key, shape, jnp.float32)
    if pieces:
        entries = entries * level_of(own_key, shape, pieces, -0.22, 0.18)
    return jnp.clip(entries, -reach, reach).astype(held_as)


def setup_inputs(seed: int = 0) -> dict:
    arg_keys = jax.random.split(jax.random.key(seed), 5)
    matrix_block = noise(arg_keys[0], (ROWS, COLS), 1.0, 6.0, ((0, 32), (1, 8)))
    sketch_matrix = noise(arg_keys[1], (COLS, SKETCH), COLS ** -0.5, 0.0390625, ((0, 8),))
    local_pivots = draw_local_pivots(jax.random.fold_in(arg_keys[4], 71), 0)
    upper_pivots = draw_upper_pivots(jax.random.fold_in(arg_keys[4], 71), 0)
    return {"matrix_block": matrix_block, "sketch_matrix": sketch_matrix, "local_pivots": local_pivots, "upper_pivots": upper_pivots}


def basis_of(stacked):
    gram_matrix = jnp.dot(stacked.T.astype(jnp.float32), stacked.astype(jnp.float32), precision=lax.Precision.HIGHEST, preferred_element_type=jnp.float32)
    lower_factor = jnp.linalg.cholesky(gram_matrix)
    solved = jax.scipy.linalg.solve_triangular(lower_factor, stacked.T, lower=True)
    return solved.T * math.sqrt(LEAF)

def select_rows(matrix_rows, indices):
    return jnp.take(matrix_rows, indices, axis=0)

def reference(matrix_block, sketch_matrix, local_pivots, upper_pivots):
    sketch_wide = sketch_matrix.astype(jnp.float32)

    def leaf_samples(block_rows):
        return jnp.dot(block_rows.astype(jnp.float32), sketch_wide, precision=lax.Precision.HIGHEST)
    sketch_product = lax.map(leaf_samples, matrix_block.reshape(2 * CLUSTERS, LEAF, COLS))
    leaf_basis = lax.map(basis_of, sketch_product).reshape(2 * CLUSTERS * LEAF, SKETCH)
    leaf_pivots = local_pivots[:, :2].reshape(2 * CLUSTERS, RANK)
    skeleton = jax.vmap(select_rows)(sketch_product, leaf_pivots)
    stacked = skeleton.reshape(CLUSTERS, 2 * RANK, SKETCH)
    device_basis = lax.map(basis_of, stacked).reshape(CLUSTERS * LEAF, SKETCH)
    current = jax.vmap(select_rows)(stacked, local_pivots[:, 2])
    tree_depth = CLUSTERS.bit_length() - 1
    level_bases = []
    for height in range(1, tree_depth + 1):
        node_count = current.shape[0] // 2
        stacked = current.reshape(node_count, 2 * RANK, SKETCH)
        level_bases.append(lax.map(basis_of, stacked))
        if height < tree_depth:
            first_row = 2 ** (tree_depth - height) - 2
            current = jax.vmap(select_rows)(stacked, upper_pivots[first_row:first_row + node_count])
    blocks_out = []
    for device_index in range(CLUSTERS):
        if device_index == 0:
            height = tree_depth
        else:
            height = (device_index & -device_index).bit_length()
        blocks_out.append(level_bases[height - 1][device_index >> height])
    inner_basis = jnp.concatenate(blocks_out, 0)
    return (leaf_basis, device_basis, inner_basis)
```

```python
import functools
import math

import jax
import jax.numpy as jnp
from jax import lax
from jax.experimental import pallas as pl
from jax.experimental.pallas import tpu as pltpu
from jax.sharding import PartitionSpec as P

HIGH = lax.Precision.HIGHEST
NT = (((1,), (1,)), ((), ()))
TN = (((0,), (0,)), ((), ()))
NN = (((1,), (0,)), ((), ()))

def mm(a, b, dims=NN):
    return lax.dot_general(a, b, dims, precision=HIGH, preferred_element_type=jnp.float32)

def row_of(x, i):
    return jnp.broadcast_to(x[:, i:i + 1, :], x.shape)

def eliminate(m_ref):
    batch = m_ref.shape[0]
    shape = (batch, 8, 128)
    sub = lax.broadcasted_iota(jnp.int32, shape, 1)
    lane = lax.broadcasted_iota(jnp.int32, shape, 2)
    zero = jnp.zeros(shape, jnp.float32)
    rows = m_ref[:, 0:8, :]
    for k in range(16):
        lo = 8 * k
        last = k == 15
        in_block = (lane >= lo) & (lane < lo + 8)
        cols = [jnp.broadcast_to(rows[:, :, lo + j:lo + j + 1], shape) for j in range(8)]
        main = jnp.where(in_block, jnp.where(lane - lo == sub, 1.0, 0.0), rows)
        if not last:
            below = m_ref[:, lo + 8:lo + 16, :]
            cols_b = [jnp.broadcast_to(below[:, :, lo + j:lo + j + 1], shape) for j in range(8)]
            nxt = jnp.where(in_block, 0.0, below)
        for j in range(8):
            scale = lax.rsqrt(row_of(cols[j], j))
            left = cols[j] * scale
            if not last:
                left_b = cols_b[j] * scale
            for i in range(j + 1, 8):
                factor = row_of(left, i)
                cols[i] = cols[i] - left * factor
                if not last:
                    cols_b[i] = cols_b[i] - left_b * factor
            pivot_row = row_of(main, j) * scale
            main = jnp.where(sub == j, pivot_row, main - jnp.where(sub > j, left, 0.0) * pivot_row)
            if not last:
                nxt = nxt - left_b * pivot_row
        m_ref[:, lo:lo + 8, :] = main
        if not last:
            rows = nxt
        if k < 14:
            rest = lo + 16
            for b in range(batch):
                panel = main[b]
                upd = lax.dot_general(panel, panel, TN, precision=HIGH, preferred_element_type=jnp.float32)
                keep = m_ref[b, rest:, :]
                lane2 = lax.broadcasted_iota(jnp.int32, keep.shape, 1)
                keep = jnp.where((lane2 >= lo) & (lane2 < lo + 8), 0.0, keep)
                m_ref[b, rest:, :] = keep - upd[rest:, :]

def kern(leaf_ref, stk_ref, up_ref, rows_ref, leaf_o, stk_o, up_o, gram, diag, tinv):
    srcs = (leaf_ref, stk_ref, up_ref)
    for b in range(3):
        w = srcs[b][...]
        for i in range(3):
            g = mm(w[128 * i:128 * i + 128], w[:128 * (i + 1)], NT)
            for j in range(i + 1):
                gram[b, i, j] = g[:, 128 * j:128 * j + 128]
    r = lax.broadcasted_iota(jnp.int32, (128, 128), 0)
    c = lax.broadcasted_iota(jnp.int32, (128, 128), 1)
    @pl.loop(0, 3)
    def _(kk):
        for b in range(3):
            diag[b] = gram[b, kk, kk]
        eliminate(diag)
        for b in range(3):
            tinv[b, kk] = jnp.where(r >= c, diag[b], 0.0)
        @pl.when(kk == 0)
        def _():
            for b in range(3):
                t = tinv[b, 0]
                l10 = mm(gram[b, 1, 0], t, NT)
                l20 = mm(gram[b, 2, 0], t, NT)
                gram[b, 1, 0] = l10
                gram[b, 2, 0] = l20
                gram[b, 1, 1] -= mm(l10, l10, NT)
                gram[b, 2, 1] -= mm(l20, l10, NT)
                gram[b, 2, 2] -= mm(l20, l20, NT)
        @pl.when(kk == 1)
        def _():
            for b in range(3):
                l21 = mm(gram[b, 2, 1], tinv[b, 1], NT)
                gram[b, 2, 1] = l21
                gram[b, 2, 2] -= mm(l21, l21, NT)
    scale = math.sqrt(512)
    outs = (leaf_o, stk_o, up_o)
    for b in range(3):
        t0, t1, t2 = tinv[b, 0], tinv[b, 1], tinv[b, 2]
        l10, l20, l21 = gram[b, 1, 0], gram[b, 2, 0], gram[b, 2, 1]
        i10 = -mm(t1, mm(l10, t0))
        i21 = -mm(t2, mm(l21, t1))
        i20 = -mm(t2, mm(l20, t0) + mm(l21, i10))
        w = rows_ref[...] if b == 0 else srcs[b][...]
        def put(i, inv):
            outs[b][:, 128 * i:128 * i + 128] = lax.dot_general(w[:128 * (i + 1)], inv * scale, (((0,), (1,)), ((), ())), precision=HIGH, preferred_element_type=jnp.float32)
        put(0, t0)
        put(1, jnp.concatenate([i10, t1], 1))
        put(2, jnp.concatenate([i20, i21, t2], 1))

def bases(leaf_t, stk_t, up_t, rows_t):
    vm = pl.BlockSpec(memory_space=pltpu.VMEM)
    return pl.pallas_call(
        kern,
        out_shape=[jax.ShapeDtypeStruct((128, 384), jnp.float32), jax.ShapeDtypeStruct((512, 384), jnp.float32), jax.ShapeDtypeStruct((512, 384), jnp.float32)],
        in_specs=[vm] * 4, out_specs=[vm] * 3,
        scratch_shapes=[pltpu.VMEM((3, 3, 3, 128, 128), jnp.float32), pltpu.VMEM((3, 128, 128), jnp.float32), pltpu.VMEM((3, 3, 128, 128), jnp.float32)],
        compiler_params=pltpu.CompilerParams(vmem_limit_bytes=48 << 20),
        name="bases",
    )(leaf_t, stk_t, up_t, rows_t)


def partner_2(block, axis, bit):
    count = lax.axis_size(axis)
    route = []
    for low in range(count):
        high = low | 1 << bit
        if high != low and high < count:
            route += [(low, high), (high, low)]
    return lax.ppermute(block, axis, route)


def select_rows(matrix_rows, indices):
    return jnp.take(matrix_rows, indices, axis=0)


def climb_tree(current, tree_depth, position, upper_pivots):
    chosen = None
    for height in range(1, tree_depth + 1):
        partner = partner_2(current, "rows", height - 1)
        on_right = position >> height - 1 & 1 == 1
        left_part = jnp.where(on_right, partner, current)
        right_part = jnp.where(on_right, current, partner)
        stacked = jnp.concatenate([left_part, right_part], 0)
        low_bits = position & (1 << height) - 1
        is_owner = low_bits == 1 << height - 1
        if height == tree_depth:
            is_owner = jnp.logical_or(is_owner, position == 0)
        chosen = stacked if chosen is None else jnp.where(is_owner, stacked, chosen)
        if height < tree_depth:
            node_row = (1 << tree_depth - height) + (position >> height) - 2
            indices = lax.dynamic_index_in_dim(upper_pivots, node_row, 0, keepdims=False)
            current = select_rows(stacked, indices)
    return chosen


def on_device(matrix_block, sketch_matrix, local_pivots, upper_pivots):
    partial_value = jnp.dot(matrix_block, sketch_matrix, preferred_element_type=jnp.float32)
    pivots = local_pivots[0]
    summed = lax.psum(partial_value, "samples")
    sample = lax.axis_index("samples")
    own_leaf = lax.dynamic_slice_in_dim(summed, (sample // 4) * 512, 512, 0)
    own_rows = lax.dynamic_slice_in_dim(summed, sample * 128, 128, 0)
    stacked = jnp.concatenate([select_rows(summed[:512], pivots[0]), select_rows(summed[512:], pivots[1])], 0)
    current = select_rows(stacked, pivots[2])
    tree_depth = lax.axis_size("rows").bit_length() - 1
    upper = climb_tree(current, tree_depth, lax.axis_index("rows"), upper_pivots)
    return tuple(bases(own_leaf.T, stacked.T, upper.T, own_rows.T))


def solution(mesh):
    in_specs = (P("rows", "samples"), P("samples", None), P("rows", None, None), P())
    out_specs = (P(("rows", "samples"), None), P("rows", None), P("rows", None))
    return jax.shard_map(
        on_device, mesh=mesh, in_specs=in_specs, out_specs=out_specs, check_vma=False
    )
```

```python
import functools
import math

import jax
import jax.numpy as jnp
from jax import lax
from jax.experimental import pallas as pl
from jax.experimental.pallas import tpu as pltpu
from jax.sharding import PartitionSpec as P

HIGH = lax.Precision.HIGHEST
NT = (((1,), (1,)), ((), ()))
TN = (((0,), (0,)), ((), ()))
NN = (((1,), (0,)), ((), ()))

def mm(a, b, dims=NN):
    return lax.dot_general(a, b, dims, precision=HIGH, preferred_element_type=jnp.float32)

def row_of(x, i):
    return jnp.broadcast_to(x[:, i:i + 1, :], x.shape)

def eliminate(m_ref):
    batch = m_ref.shape[0]
    shape = (batch, 8, 128)
    sub = lax.broadcasted_iota(jnp.int32, shape, 1)
    lane = lax.broadcasted_iota(jnp.int32, shape, 2)
    zero = jnp.zeros(shape, jnp.float32)
    rows = m_ref[:, 0:8, :]
    for k in range(16):
        lo = 8 * k
        last = k == 15
        in_block = (lane >= lo) & (lane < lo + 8)
        cols = [jnp.broadcast_to(rows[:, :, lo + j:lo + j + 1], shape) for j in range(8)]
        main = jnp.where(in_block, jnp.where(lane - lo == sub, 1.0, 0.0), rows)
        if not last:
            below = m_ref[:, lo + 8:lo + 16, :]
            cols_b = [jnp.broadcast_to(below[:, :, lo + j:lo + j + 1], shape) for j in range(8)]
            nxt = jnp.where(in_block, 0.0, below)
        for j in range(8):
            scale = lax.rsqrt(row_of(cols[j], j))
            left = cols[j] * scale
            if not last:
                left_b = cols_b[j] * scale
            for i in range(j + 1, 8):
                factor = row_of(left, i)
                cols[i] = cols[i] - left * factor
                if not last:
                    cols_b[i] = cols_b[i] - left_b * factor
            pivot_row = row_of(main, j) * scale
            main = jnp.where(sub == j, pivot_row, main - jnp.where(sub > j, left, 0.0) * pivot_row)
            if not last:
                nxt = nxt - left_b * pivot_row
        m_ref[:, lo:lo + 8, :] = main
        if not last:
            rows = nxt
        if k < 14:
            rest = lo + 16
            for b in range(batch):
                panel = main[b]
                upd = lax.dot_general(panel, panel, TN, precision=HIGH, preferred_element_type=jnp.float32)
                keep = m_ref[b, rest:, :]
                lane2 = lax.broadcasted_iota(jnp.int32, keep.shape, 1)
                keep = jnp.where((lane2 >= lo) & (lane2 < lo + 8), 0.0, keep)
                m_ref[b, rest:, :] = keep - upd[rest:, :]

def kern(leaf_ref, stk_ref, up_ref, leaf_o, stk_o, up_o, gram, diag, tinv):
    srcs = (leaf_ref, stk_ref, up_ref)
    for b in range(3):
        w = srcs[b][...]
        for i in range(3):
            g = mm(w[128 * i:128 * i + 128], w[:128 * (i + 1)], NT)
            for j in range(i + 1):
                gram[b, i, j] = g[:, 128 * j:128 * j + 128]
    r = lax.broadcasted_iota(jnp.int32, (128, 128), 0)
    c = lax.broadcasted_iota(jnp.int32, (128, 128), 1)
    @pl.loop(0, 3)
    def _(kk):
        for b in range(3):
            diag[b] = gram[b, kk, kk]
        eliminate(diag)
        for b in range(3):
            tinv[b, kk] = jnp.where(r >= c, diag[b], 0.0)
        @pl.when(kk == 0)
        def _():
            for b in range(3):
                t = tinv[b, 0]
                l10 = mm(gram[b, 1, 0], t, NT)
                l20 = mm(gram[b, 2, 0], t, NT)
                gram[b, 1, 0] = l10
                gram[b, 2, 0] = l20
                gram[b, 1, 1] -= mm(l10, l10, NT)
                gram[b, 2, 1] -= mm(l20, l10, NT)
                gram[b, 2, 2] -= mm(l20, l20, NT)
        @pl.when(kk == 1)
        def _():
            for b in range(3):
                l21 = mm(gram[b, 2, 1], tinv[b, 1], NT)
                gram[b, 2, 1] = l21
                gram[b, 2, 2] -= mm(l21, l21, NT)
    scale = math.sqrt(512)
    share = pl.ds(pl.multiple_of((lax.axis_index("samples") % 4) * 128, 128), 128)
    outs = (leaf_o, stk_o, up_o)
    for b in range(3):
        t0, t1, t2 = tinv[b, 0], tinv[b, 1], tinv[b, 2]
        l10, l20, l21 = gram[b, 1, 0], gram[b, 2, 0], gram[b, 2, 1]
        i10 = -mm(t1, mm(l10, t0))
        i21 = -mm(t2, mm(l21, t1))
        i20 = -mm(t2, mm(l20, t0) + mm(l21, i10))
        w = leaf_ref[:, share] if b == 0 else srcs[b][...]
        def put(i, inv):
            outs[b][:, 128 * i:128 * i + 128] = lax.dot_general(w[:128 * (i + 1)], inv * scale, (((0,), (1,)), ((), ())), precision=HIGH, preferred_element_type=jnp.float32)
        put(0, t0)
        put(1, jnp.concatenate([i10, t1], 1))
        put(2, jnp.concatenate([i20, i21, t2], 1))

def bases(leaf_t, stk_t, up_t):
    vm = pl.BlockSpec(memory_space=pltpu.VMEM)
    return pl.pallas_call(
        kern,
        out_shape=[jax.ShapeDtypeStruct((128, 384), jnp.float32), jax.ShapeDtypeStruct((512, 384), jnp.float32), jax.ShapeDtypeStruct((512, 384), jnp.float32)],
        in_specs=[vm] * 3, out_specs=[vm] * 3,
        scratch_shapes=[pltpu.VMEM((3, 3, 3, 128, 128), jnp.float32), pltpu.VMEM((3, 128, 128), jnp.float32), pltpu.VMEM((3, 3, 128, 128), jnp.float32)],
        compiler_params=pltpu.CompilerParams(vmem_limit_bytes=48 << 20),
        name="bases",
    )(leaf_t, stk_t, up_t)


MESH = pl.DeviceIdType.MESH
SHARE = 48
HALF = 192


def pick(values, indices):
    high = values.astype(jnp.bfloat16)
    rest = values - high.astype(jnp.float32)
    middle = rest.astype(jnp.bfloat16)
    low = (rest - middle.astype(jnp.float32)).astype(jnp.bfloat16)
    terms = jnp.concatenate([high, middle, low], 0)
    rows = lax.broadcasted_iota(jnp.int32, (values.shape[1], indices.shape[1]), 0)
    chosen = jnp.where(rows == indices, 1.0, 0.0).astype(jnp.bfloat16)
    found = jnp.dot(terms, chosen, preferred_element_type=jnp.float32)
    count = values.shape[0]
    return found[:count] + found[count:2 * count] + found[2 * count:]


def exchange(pt_ref, piv_ref, node_ref, leaf_ref, stk_ref, up_ref,
             swap, half_sum, parts, own, own_stk, below, climb_in, climb_out,
             swap_send, swap_recv, part_send, part_recv, gather_send, gather_recv,
             pair_send, pair_recv, tree_send, tree_recv):
    r = lax.axis_index("rows")
    s = lax.axis_index("samples")
    x = s // 2
    c = s % 2
    twin = s + 1 - 2 * c
    level2 = (r % 4) == 2
    level3 = (r % 8) == 4
    level4 = (r % 16) == 8
    odd = (r % 2) == 1
    root = (r % 16) == 0

    def peer(d):
        return ((x + d) % 4) * 2 + c

    def at(row, sample):
        return (row, sample)

    barrier = pltpu.get_barrier_semaphore()

    def greet(row, sample):
        pl.semaphore_signal(barrier, inc=1, device_id=at(row, sample), device_id_type=MESH)

    greet(r, twin)
    for d in range(1, 4):
        greet(r, peer(d))
    step = jnp.where(level2, 1, jnp.where(level3, 2, jnp.where(level4, 4, 8)))

    @pl.when(odd)
    def _():
        greet(r - 1, s)

    @pl.when(jnp.logical_not(odd))
    def _():
        greet(jnp.where(r == 0, 8, r - step), s)
        greet(jnp.where(r == 0, 24, r + step), s)

    even = jnp.where(odd, 0, 1)
    pl.semaphore_wait(barrier, 4 + even + jnp.where(root, 0, 1) + jnp.where(level4, 1, 0))

    def swap_copy(h):
        return pltpu.make_async_remote_copy(
            src_ref=pt_ref.at[pl.ds(pl.multiple_of(HALF * (1 - c), 8), HALF), pl.ds(512 * h, 512)],
            dst_ref=swap.at[h],
            send_sem=swap_send.at[h], recv_sem=swap_recv.at[h],
            device_id=at(r, twin), device_id_type=MESH)

    swap_copy(0).start()
    swap_copy(1).start()

    def part_copy(h, d):
        return pltpu.make_async_remote_copy(
            src_ref=half_sum.at[h, pl.ds(pl.multiple_of(SHARE * ((x + d) % 4), 8), SHARE), :],
            dst_ref=parts.at[h, d - 1],
            send_sem=part_send.at[h, d - 1], recv_sem=part_recv.at[h, d - 1],
            device_id=at(r, peer(d)), device_id_type=MESH)

    for h in range(2):
        swap_copy(h).wait_recv()
        half_sum[h] = pt_ref[pl.ds(pl.multiple_of(HALF * c, 8), HALF), 512 * h:512 * h + 512] + swap[h]
        for d in (2, 1, 3):
            part_copy(h, d).start()
    my_rows = pl.ds(pl.multiple_of(SHARE * x, 8), SHARE)
    my_place = pl.ds(pl.multiple_of(HALF * c + SHARE * x, 8), SHARE)
    my_half = pl.ds(pl.multiple_of(HALF * c, 8), HALF)

    def gather_copy(n, d):
        out = (leaf_ref, stk_ref, up_ref)[n]
        src = (own.at[((x + d) % 4) // 2], own_stk, climb_in)[n]
        return pltpu.make_async_remote_copy(
            src_ref=src, dst_ref=out.at[my_place, :],
            send_sem=gather_send.at[n, d - 1], recv_sem=gather_recv.at[n, d - 1],
            device_id=at(r, peer(d)), device_id_type=MESH)

    def pair_copy(n):
        out = (leaf_ref, stk_ref, up_ref)[n]
        return pltpu.make_async_remote_copy(
            src_ref=out.at[my_half, :], dst_ref=out.at[my_half, :],
            send_sem=pair_send.at[n], recv_sem=pair_recv.at[n],
            device_id=at(r, twin), device_id_type=MESH)

    for h in range(2):
        for d in (1, 3, 2):
            part_copy(h, d).wait_recv()
        total = half_sum[h, my_rows, :] + parts[h, 0] + parts[h, 1] + parts[h, 2]
        own[h] = total
        own_stk[:, 256 * h:256 * h + 256] = pick(total, piv_ref[h:h + 1, :])
    stacked = own_stk[...]
    skeleton = pick(stacked, piv_ref[2:3, :])

    def skeleton_copy():
        return pltpu.make_async_remote_copy(
            src_ref=below, dst_ref=climb_in.at[:, pl.ds(0, 256)],
            send_sem=tree_send.at[0], recv_sem=tree_recv.at[0],
            device_id=at(r + 1, s), device_id_type=MESH)

    @pl.when(odd)
    def _():
        climb_in[:, 256:] = skeleton

    @pl.when(jnp.logical_not(odd))
    def _():
        below[...] = skeleton
        skeleton_copy().start()

    leaf_ref[my_place, :] = own[x // 2]
    stk_ref[my_place, :] = stacked
    for n in range(2):
        for d in (2, 1, 3):
            gather_copy(n, d).start()

    width = jnp.where(odd, 2, 2 * (2 * step))
    side = (r // width) % 2
    reach = width // 2
    parent = jnp.where(side == 0, r + reach, r - reach)

    def tree_copy(to, sem):
        return pltpu.make_async_remote_copy(
            src_ref=climb_out,
            dst_ref=climb_in.at[:, pl.ds(pl.multiple_of(256 * side, 128), 256)],
            send_sem=tree_send.at[sem], recv_sem=tree_recv.at[side],
            device_id=at(to, s), device_id_type=MESH)

    def arrived(half):
        return pltpu.make_async_remote_copy(
            src_ref=climb_out, dst_ref=climb_in.at[:, pl.ds(256 * half, 256)],
            send_sem=tree_send.at[1], recv_sem=tree_recv.at[half],
            device_id=at(r, twin), device_id_type=MESH)

    arrived(0).wait_recv()

    @pl.when(jnp.logical_not(odd))
    def _():
        arrived(1).wait_recv()

    @pl.when(jnp.logical_not(root))
    def _():
        climb_out[...] = pick(climb_in[...], node_ref[...])
        tree_copy(parent, 1).start()

    @pl.when(level4)
    def _():
        tree_copy(0, 2).start()

    up_ref[my_place, :] = climb_in[...]
    for d in (2, 1, 3):
        gather_copy(2, d).start()
    for n in range(3):
        for d in (1, 3, 2):
            gather_copy(n, d).wait_recv()
        pair_copy(n).start()
    for h in range(2):
        swap_copy(h).wait_send()
        for d in range(1, 4):
            part_copy(h, d).wait_send()
    for n in range(3):
        for d in range(1, 4):
            gather_copy(n, d).wait_send()

    @pl.when(jnp.logical_not(odd))
    def _():
        skeleton_copy().wait_send()

    @pl.when(jnp.logical_not(root))
    def _():
        tree_copy(parent, 1).wait_send()

    @pl.when(level4)
    def _():
        tree_copy(0, 2).wait_send()

    for n in range(3):
        pair_copy(n).wait()


def gathered(partial_t, pivots, node_pivots):
    vmem = pl.BlockSpec(memory_space=pltpu.VMEM)
    f32 = jnp.float32
    dma = pltpu.SemaphoreType.DMA
    return pl.pallas_call(
        exchange,
        out_shape=[jax.ShapeDtypeStruct((384, 512), f32)] * 3,
        in_specs=[vmem] * 3, out_specs=[vmem] * 3,
        scratch_shapes=[
            pltpu.VMEM((2, HALF, 512), f32), pltpu.VMEM((2, HALF, 512), f32),
            pltpu.VMEM((2, 3, SHARE, 512), f32), pltpu.VMEM((2, SHARE, 512), f32),
            pltpu.VMEM((SHARE, 512), f32), pltpu.VMEM((SHARE, 256), f32),
            pltpu.VMEM((SHARE, 512), f32), pltpu.VMEM((SHARE, 256), f32),
            dma((2,)), dma((2,)), dma((2, 3)), dma((2, 3)), dma((3, 3)), dma((3, 3)),
            dma((3,)), dma((3,)), dma((3,)), dma((2,)),
        ],
        compiler_params=pltpu.CompilerParams(collective_id=0, has_side_effects=True, vmem_limit_bytes=48 << 20),
        name="exchange",
    )(partial_t, pivots, node_pivots)


def on_device(matrix_block, sketch_matrix, local_pivots, upper_pivots):
    partial_t = lax.dot_general(
        sketch_matrix, matrix_block, (((0,), (1,)), ((), ())), preferred_element_type=jnp.float32)
    table = []
    for r in range(32):
        level = 5 if r == 0 else (r & -r).bit_length()
        table.append(0 if level == 5 else 2 ** (5 - level) + (r >> level) - 2)
    node_row = jnp.asarray(table, jnp.int32)[lax.axis_index("rows")]
    node_pivots = lax.dynamic_slice_in_dim(upper_pivots, node_row, 1, 0)
    return tuple(bases(*gathered(partial_t, local_pivots[0], node_pivots)))


def solution(mesh):
    in_specs = (P("rows", "samples"), P("samples", None), P("rows", None, None), P())
    out_specs = (P(("rows", "samples"), None), P("rows", None), P("rows", None))
    return jax.shard_map(
        on_device, mesh=mesh, in_specs=in_specs, out_specs=out_specs, check_vma=False
    )
```

```python
import math

import jax
import jax.numpy as jnp
from jax import lax
from jax.experimental import pallas as pl
from jax.experimental.pallas import tpu as pltpu
from jax.sharding import PartitionSpec as P

SUBS = 4
NN = (((1,), (0,)), ((), ()))
NT = (((1,), (1,)), ((), ()))
TN = (((0,), (0,)), ((), ()))
TT = (((0,), (1,)), ((), ()))

def mm(a, b, dims):
    return lax.dot_general(a, b, dims, precision=lax.Precision.HIGH, preferred_element_type=jnp.float32)

def row_of(x, i):
    return jnp.broadcast_to(x[:, i:i + 1, :], x.shape)

def eliminate(m_ref):
    batch = m_ref.shape[0]
    shape = (batch, 8, 128)
    sub = lax.broadcasted_iota(jnp.int32, shape, 1)
    lane = lax.broadcasted_iota(jnp.int32, shape, 2)
    span = 8 * SUBS
    for start in range(0, 128, span):
        groups = [m_ref[:, start + 8 * g:start + 8 * g + 8, :] for g in range(SUBS)]
        for q in range(SUBS):
            lo = start + 8 * q
            in_block = (lane >= lo) & (lane < lo + 8)
            cols = [None] * q + [[jnp.broadcast_to(groups[g][:, :, lo + j:lo + j + 1], shape) for j in range(8)] for g in range(q, SUBS)]
            groups[q] = jnp.where(in_block, jnp.where(lane - lo == sub, 1.0, 0.0), groups[q])
            for g in range(q + 1, SUBS):
                groups[g] = jnp.where(in_block, 0.0, groups[g])
            pivot = row_of(cols[q][0], 0)
            for j in range(8):
                scale = lax.rsqrt(pivot)
                inverse = scale * scale
                own = cols[q]
                column = own[j]
                if j < 7:
                    raw = row_of(column, j + 1)
                    pivot = row_of(own[j + 1], j + 1) - (raw * raw) * inverse
                for i in range(j + 1, 8):
                    factor = row_of(column, i) * inverse
                    for g in range(q, SUBS):
                        cols[g][i] = cols[g][i] - cols[g][j] * factor
                base = row_of(groups[q], j)
                scaled = base * inverse
                groups[q] = jnp.where(sub == j, base * scale, groups[q] - jnp.where(sub > j, column, 0.0) * scaled)
                for g in range(q + 1, SUBS):
                    groups[g] = groups[g] - cols[g][j] * scaled
        for g in range(SUBS):
            m_ref[:, start + 8 * g:start + 8 * g + 8, :] = groups[g]
        rest = start + span
        if rest < 128:
            for b in range(batch):
                panel = jnp.concatenate([groups[g][b] for g in range(SUBS)], 0)
                prow = lax.broadcasted_iota(jnp.int32, panel.shape, 0)
                plane = lax.broadcasted_iota(jnp.int32, panel.shape, 1)
                done = jnp.where((plane >= start) & (plane < rest) & (plane - start >= (prow // 8) * 8 + 8), 0.0, panel)
                upd = mm(panel, done, TN)
                keep = m_ref[b, rest:, :]
                lane2 = lax.broadcasted_iota(jnp.int32, keep.shape, 1)
                keep = jnp.where((lane2 >= start) & (lane2 < rest), 0.0, keep)
                m_ref[b, rest:, :] = keep - upd[rest:, :]

def factor(leaf_ref, stk_ref, up_ref, leaf_o, stk_o, up_o, diag):
    srcs = (leaf_ref, stk_ref, up_ref)
    outs = (leaf_o, stk_o, up_o)
    share = pl.ds(pl.multiple_of((lax.axis_index("samples") % 4) * 128, 128), 128)
    r = lax.broadcasted_iota(jnp.int32, (128, 128), 0)
    c = lax.broadcasted_iota(jnp.int32, (128, 128), 1)
    lower = r >= c
    scale = math.sqrt(512)
    def blk(b, i):
        return srcs[b][128 * i:128 * i + 128, :]
    def rows(b, i):
        return leaf_ref[128 * i:128 * i + 128, share] if b == 0 else blk(b, i)
    B = range(3)
    for b in B:
        diag[0, b] = mm(blk(b, 0), blk(b, 0), NT)
    g10 = [mm(blk(b, 1), blk(b, 0), NT) for b in B]
    g20 = [mm(blk(b, 2), blk(b, 0), NT) for b in B]
    g11 = [mm(blk(b, 1), blk(b, 1), NT) for b in B]
    g21 = [mm(blk(b, 2), blk(b, 1), NT) for b in B]
    g22 = [mm(blk(b, 2), blk(b, 2), NT) for b in B]
    eliminate(diag.at[0])
    t0 = [jnp.where(lower, diag[0, b], 0.0) for b in B]
    l10 = [mm(g10[b], t0[b], NT) for b in B]
    for b in B:
        diag[1, b] = g11[b] - mm(l10[b], l10[b], NT)
    l20 = [mm(g20[b], t0[b], NT) for b in B]
    g21 = [g21[b] - mm(l20[b], l10[b], NT) for b in B]
    g22 = [g22[b] - mm(l20[b], l20[b], NT) for b in B]
    x0 = [mm(rows(b, 0), t0[b] * scale, TT) for b in B]
    for b in B:
        outs[b][:, :128] = x0[b]
    l10s = [l10[b] * (1 / scale) for b in B]
    l20s = [l20[b] * (1 / scale) for b in B]
    y1 = [rows(b, 1).T - mm(x0[b], l10s[b], NT) for b in B]
    y2 = [rows(b, 2).T - mm(x0[b], l20s[b], NT) for b in B]
    eliminate(diag.at[1])
    t1 = [jnp.where(lower, diag[1, b], 0.0) for b in B]
    l21 = [mm(g21[b], t1[b], NT) for b in B]
    for b in B:
        diag[2, b] = g22[b] - mm(l21[b], l21[b], NT)
    x1 = [mm(y1[b], t1[b] * scale, NT) for b in B]
    for b in B:
        outs[b][:, 128:256] = x1[b]
    y2 = [y2[b] - mm(x1[b], l21[b] * (1 / scale), NT) for b in B]
    eliminate(diag.at[2])
    t2 = [jnp.where(lower, diag[2, b], 0.0) for b in B]
    for b in B:
        outs[b][:, 256:] = mm(y2[b], t2[b] * scale, NT)

def bases(leaf_t, stk_t, up_t):
    vm = pl.BlockSpec(memory_space=pltpu.VMEM)
    f32 = jnp.float32
    return pl.pallas_call(
        factor,
        out_shape=[jax.ShapeDtypeStruct((128, 384), f32), jax.ShapeDtypeStruct((512, 384), f32), jax.ShapeDtypeStruct((512, 384), f32)],
        in_specs=[vm] * 3, out_specs=[vm] * 3,
        scratch_shapes=[pltpu.VMEM((3, 3, 128, 128), f32)],
        compiler_params=pltpu.CompilerParams(vmem_limit_bytes=48 << 20),
        name="bases",
    )(leaf_t, stk_t, up_t)


MESH = pl.DeviceIdType.MESH
SHARE = 48
HALF = 192
PART = 24


def pick(values, indices):
    high = values.astype(jnp.bfloat16)
    rest = values - high.astype(jnp.float32)
    middle = rest.astype(jnp.bfloat16)
    low = (rest - middle.astype(jnp.float32)).astype(jnp.bfloat16)
    terms = jnp.concatenate([high, middle, low], 0)
    rows = lax.broadcasted_iota(jnp.int32, (values.shape[1], indices.shape[1]), 0)
    chosen = jnp.where(rows == indices, 1.0, 0.0).astype(jnp.bfloat16)
    found = jnp.dot(terms, chosen, preferred_element_type=jnp.float32)
    count = values.shape[0]
    return found[:count] + found[count:2 * count] + found[2 * count:]


def exchange(pt_ref, piv_ref, node_ref, leaf_ref, stk_ref, up_ref,
             swap, half_sum, passing, parts, own, own_stk, below, climb_in, climb_out, extra_in, extra_out,
             swap_send, swap_recv, pass_send, pass_recv, part_send, part_recv, direct_send, direct_recv,
             relay_send, relay_recv, pair_send, pair_recv, tree_send, tree_recv, extra_recv):
    r = lax.axis_index("rows")
    s = lax.axis_index("samples")
    x = s // 2
    c = s % 2
    twin = s + 1 - 2 * c
    beside = (((x + 1) % 4) * 2 + c, ((x + 3) % 4) * 2 + c)
    odd = (r % 2) == 1
    even = jnp.logical_not(odd)
    level2 = (r % 4) == 2
    helper = (r % 8) == 0
    level4 = (r % 16) == 8
    root = (r % 16) == 0

    barrier = pltpu.get_barrier_semaphore()

    def greet(row, sample):
        pl.semaphore_signal(barrier, inc=1, device_id=(row, sample), device_id_type=MESH)

    def send(src, dst, sems, to):
        return pltpu.make_async_remote_copy(
            src_ref=src, dst_ref=dst, send_sem=sems[0], recv_sem=sems[1], device_id=to, device_id_type=MESH)

    greet(r, twin)
    greet(r, beside[0])
    greet(r, beside[1])

    @pl.when(odd)
    def _():
        greet(r - 1, s)

    @pl.when(even)
    def _():
        greet(jnp.where(helper, r + 2, jnp.where(level2, r - 1, r - 2)), s)
        greet(jnp.where(helper, r + 6, jnp.where(level2, r + 1, r + 2)), s)

    @pl.when(level4)
    def _():
        greet(r - 8, s)

    @pl.when(root)
    def _():
        greet(8, s)
        greet(24, s)

    pl.semaphore_wait(
        barrier, 4 + jnp.where(level2, 2, 0) + jnp.where(helper, 1, 0) + jnp.where(level4, 1, 0))

    def swap_copy(h):
        return send(
            pt_ref.at[pl.ds(pl.multiple_of(HALF * (1 - c), 8), HALF), pl.ds(512 * h, 512)], swap.at[h],
            (swap_send.at[h], swap_recv.at[h]), (r, twin))

    swap_copy(0).start()
    swap_copy(1).start()

    def share(d, first=0, count=SHARE):
        return pl.ds(pl.multiple_of(SHARE * ((x + d) % 4) + first, 8), count)

    def pass_copy(h, way):
        return send(
            half_sum.at[h, share(2, PART * way, PART), :], passing.at[h, way],
            (pass_send.at[h, way], pass_recv.at[h, way]), (r, beside[way]))

    def part_copy(h, way):
        return send(
            half_sum.at[h, share((1, 3)[way]), :], parts.at[h, way],
            (part_send.at[h, way], part_recv.at[h, way]), (r, beside[way]))

    for h in range(2):
        swap_copy(h).wait_recv()
        half_sum[h] = pt_ref[pl.ds(pl.multiple_of(HALF * c, 8), HALF), 512 * h:512 * h + 512] + swap[h]
        for way in range(2):
            pass_copy(h, way).start()
    for h in range(2):
        for way in range(2):
            pass_copy(h, way).wait_recv()
            mine = share((1, 3)[way], PART * way, PART)
            half_sum[h, mine, :] += passing[h, way]
            part_copy(h, way).start()

    def place(d, first=0, count=SHARE):
        return pl.ds(pl.multiple_of(HALF * c + SHARE * ((x + d) % 4) + first, 8), count)

    outs = (leaf_ref, stk_ref, up_ref)
    OFFSET = (1, 3)

    def direct_copy(n, way):
        src = (own.at[((x + OFFSET[way]) % 4) // 2], own_stk, climb_in)[n]
        return send(
            src, outs[n].at[place(0), :], (direct_send.at[n, way], direct_recv.at[n, way]), (r, beside[way]))

    def relay_copy(n, way):
        back = OFFSET[1 - way]
        region = outs[n].at[place(back, PART * way, PART), :]
        return send(region, region, (relay_send.at[n, way], relay_recv.at[n, way]), (r, beside[way]))

    first_of_pair = (x % 2) == 0
    mate = jnp.where(first_of_pair, beside[0], beside[1])

    def leaf_relay():
        region = leaf_ref.at[place(jnp.where(first_of_pair, 3, 1)), :]
        return send(region, region, (relay_send.at[0, 0], relay_recv.at[0, 0]), (r, mate))

    def pair_copy(n, d):
        region = outs[n].at[place(d), :]
        return send(region, region, (pair_send.at[n, d], pair_recv.at[n, d]), (r, twin))

    def spread(n):
        for way in range(2):
            direct_copy(n, way).start()
        pair_copy(n, 0).start()

    def collect(n):
        for way in range(2):
            direct_copy(n, way).wait_recv()
            if n > 0:
                relay_copy(n, way).start()
            pair_copy(n, OFFSET[1 - way]).start()
        if n == 0:
            leaf_relay().start()

    def finish(n):
        if n == 0:
            leaf_relay().wait_recv()
        else:
            for way in range(2):
                relay_copy(n, way).wait_recv()
        pair_copy(n, 2).start()

    for h in range(2):
        for way in range(2):
            part_copy(h, way).wait_recv()
        total = half_sum[h, share(0), :] + parts[h, 0] + parts[h, 1]
        own[h] = total
        own_stk[:, 256 * h:256 * h + 256] = pick(total, piv_ref[0, h:h + 1, :])
    stacked = own_stk[...]
    skeleton = pick(stacked, piv_ref[0, 2:3, :])

    def skeleton_copy():
        return send(below, climb_in.at[:, pl.ds(0, 256)], (tree_send.at[0], tree_recv.at[0]), (r + 1, s))

    @pl.when(odd)
    def _():
        climb_in[:, 256:] = skeleton

    @pl.when(even)
    def _():
        below[...] = skeleton
        skeleton_copy().start()

    leaf_ref[place(0), :] = own[x // 2]
    stk_ref[place(0), :] = stacked

    node_row = jnp.where(odd, 14 + r // 2, jnp.where(level2, 6 + r // 4, r // 16))
    side = jnp.where(odd, (r // 2) % 2, jnp.where(level2, (r // 4) % 2, r // 16))
    where_to = pl.ds(pl.multiple_of(256 * side, 128), 256)

    def tree_copy(to, sem):
        return send(climb_out, climb_in.at[:, where_to], (tree_send.at[sem], tree_recv.at[side]), (to, s))

    def aside_copy():
        return send(climb_out, extra_in.at[:, where_to], (tree_send.at[2], extra_recv.at[side]), (r - r % 8, s))

    def extra_copy():
        return send(extra_out, climb_in.at[:, pl.ds(0, 256)], (tree_send.at[3], tree_recv.at[0]), (r + 8, s))

    def arrived(buffer, sems, half):
        send(climb_out, buffer.at[:, pl.ds(256 * half, 256)], (tree_send.at[1], sems.at[half]), (r, twin)).wait_recv()

    def select():
        climb_out[...] = pick(climb_in[...], node_ref[pl.ds(node_row, 1), :])

    up_one = jnp.where(side == 0, r + 1, r - 1)
    up_two = jnp.where(side == 0, r + 2, r - 2)

    @pl.when(odd)
    def _():
        arrived(climb_in, tree_recv, 0)
        select()
        tree_copy(up_one, 1).start()

    spread(0)
    spread(1)

    @pl.when(level2)
    def _():
        arrived(climb_in, tree_recv, 0)
        arrived(climb_in, tree_recv, 1)
        select()
        aside_copy().start()
        tree_copy(up_two, 1).start()

    collect(0)
    collect(1)

    @pl.when(helper)
    def _():
        arrived(extra_in, extra_recv, 0)
        arrived(extra_in, extra_recv, 1)
        extra_out[...] = pick(extra_in[...], node_ref[pl.ds(2 + r // 8, 1), :])

    @pl.when(level4)
    def _():
        climb_in[:, 256:] = extra_out[...]
        arrived(climb_in, tree_recv, 0)
        select()
        tree_copy(16, 1).start()
        tree_copy(0, 2).start()

    @pl.when(root)
    def _():
        extra_copy().start()

    @pl.when(jnp.logical_or(root, (r % 8) == 4))
    def _():
        arrived(climb_in, tree_recv, 0)
        arrived(climb_in, tree_recv, 1)

    up_ref[place(0), :] = climb_in[...]
    spread(2)
    finish(0)
    finish(1)
    collect(2)
    finish(2)

    for h in range(2):
        swap_copy(h).wait_send()
        for way in range(2):
            pass_copy(h, way).wait_send()
            part_copy(h, way).wait_send()

    @pl.when(even)
    def _():
        skeleton_copy().wait_send()

    @pl.when(odd)
    def _():
        tree_copy(up_one, 1).wait_send()

    @pl.when(level2)
    def _():
        aside_copy().wait_send()
        tree_copy(up_two, 1).wait_send()

    @pl.when(root)
    def _():
        extra_copy().wait_send()

    @pl.when(level4)
    def _():
        tree_copy(16, 1).wait_send()
        tree_copy(0, 2).wait_send()

    leaf_relay().wait_send()
    for n in range(3):
        for way in range(2):
            direct_copy(n, way).wait_send()
            if n > 0:
                relay_copy(n, way).wait_send()
        for d in range(4):
            pair_copy(n, d).wait()


def gathered(partial_t, pivots, node_pivots):
    vmem = pl.BlockSpec(memory_space=pltpu.VMEM)
    f32 = jnp.float32
    dma = pltpu.SemaphoreType.DMA
    return pl.pallas_call(
        exchange,
        out_shape=[jax.ShapeDtypeStruct((384, 512), f32)] * 3,
        in_specs=[vmem] * 3, out_specs=[vmem] * 3,
        scratch_shapes=[
            pltpu.VMEM((2, HALF, 512), f32), pltpu.VMEM((2, HALF, 512), f32),
            pltpu.VMEM((2, 2, PART, 512), f32), pltpu.VMEM((2, 2, SHARE, 512), f32),
            pltpu.VMEM((2, SHARE, 512), f32), pltpu.VMEM((SHARE, 512), f32), pltpu.VMEM((SHARE, 256), f32),
            pltpu.VMEM((SHARE, 512), f32), pltpu.VMEM((SHARE, 256), f32),
            pltpu.VMEM((SHARE, 512), f32), pltpu.VMEM((SHARE, 256), f32),
            dma((2,)), dma((2,)), dma((2, 2)), dma((2, 2)), dma((2, 2)), dma((2, 2)), dma((3, 2)), dma((3, 2)),
            dma((3, 2)), dma((3, 2)), dma((3, 4)), dma((3, 4)), dma((4,)), dma((2,)), dma((2,)),
        ],
        compiler_params=pltpu.CompilerParams(collective_id=0, has_side_effects=True, vmem_limit_bytes=48 << 20),
        name="exchange",
    )(partial_t, pivots, node_pivots)


def on_device(matrix_block, sketch_matrix, local_pivots, upper_pivots):
    partial_t = lax.dot_general(
        sketch_matrix, matrix_block, (((0,), (1,)), ((), ())), preferred_element_type=jnp.float32)
    return tuple(bases(*gathered(partial_t, local_pivots, upper_pivots)))


def solution(mesh):
    in_specs = (P("rows", "samples"), P("samples", None), P("rows", None, None), P())
    out_specs = (P(("rows", "samples"), None), P("rows", None), P("rows", None))
    return jax.shard_map(
        on_device, mesh=mesh, in_specs=in_specs, out_specs=out_specs, check_vma=False
    )
```

```python
import math

import jax
import jax.numpy as jnp
from jax import lax
from jax.experimental import pallas as pl
from jax.experimental.pallas import tpu as pltpu
from jax.sharding import PartitionSpec as P

SUBS = 4
NN = (((1,), (0,)), ((), ()))
NT = (((1,), (1,)), ((), ()))
TN = (((0,), (0,)), ((), ()))
TT = (((0,), (1,)), ((), ()))

def mm(a, b, dims):
    return lax.dot_general(a, b, dims, precision=lax.Precision.HIGH, preferred_element_type=jnp.float32)

def row_of(x, i):
    return jnp.broadcast_to(x[:, i:i + 1, :], x.shape)

def eliminate(m_ref):
    batch = m_ref.shape[0]
    shape = (batch, 8, 128)
    sub = lax.broadcasted_iota(jnp.int32, shape, 1)
    lane = lax.broadcasted_iota(jnp.int32, shape, 2)
    span = 8 * SUBS
    for start in range(0, 128, span):
        groups = [m_ref[:, start + 8 * g:start + 8 * g + 8, :] for g in range(SUBS)]
        for q in range(SUBS):
            lo = start + 8 * q
            in_block = (lane >= lo) & (lane < lo + 8)
            cols = [None] * q + [[jnp.broadcast_to(groups[g][:, :, lo + j:lo + j + 1], shape) for j in range(8)] for g in range(q, SUBS)]
            groups[q] = jnp.where(in_block, jnp.where(lane - lo == sub, 1.0, 0.0), groups[q])
            for g in range(q + 1, SUBS):
                groups[g] = jnp.where(in_block, 0.0, groups[g])
            pivot = row_of(cols[q][0], 0)
            for j in range(8):
                scale = lax.rsqrt(pivot)
                inverse = scale * scale
                own = cols[q]
                column = own[j]
                if j < 7:
                    raw = row_of(column, j + 1)
                    pivot = row_of(own[j + 1], j + 1) - (raw * raw) * inverse
                for i in range(j + 1, 8):
                    factor = row_of(column, i) * inverse
                    for g in range(q, SUBS):
                        cols[g][i] = cols[g][i] - cols[g][j] * factor
                base = row_of(groups[q], j)
                scaled = base * inverse
                groups[q] = jnp.where(sub == j, base * scale, groups[q] - jnp.where(sub > j, column, 0.0) * scaled)
                for g in range(q + 1, SUBS):
                    groups[g] = groups[g] - cols[g][j] * scaled
        for g in range(SUBS):
            m_ref[:, start + 8 * g:start + 8 * g + 8, :] = groups[g]
        rest = start + span
        if rest < 128:
            for b in range(batch):
                panel = jnp.concatenate([groups[g][b] for g in range(SUBS)], 0)
                prow = lax.broadcasted_iota(jnp.int32, panel.shape, 0)
                plane = lax.broadcasted_iota(jnp.int32, panel.shape, 1)
                done = jnp.where((plane >= start) & (plane < rest) & (plane - start >= (prow // 8) * 8 + 8), 0.0, panel)
                upd = mm(panel, done, TN)
                keep = m_ref[b, rest:, :]
                lane2 = lax.broadcasted_iota(jnp.int32, keep.shape, 1)
                keep = jnp.where((lane2 >= start) & (lane2 < rest), 0.0, keep)
                m_ref[b, rest:, :] = keep - upd[rest:, :]

def factor(leaf_ref, stk_ref, up_ref, leaf_o, stk_o, up_o, diag):
    srcs = (leaf_ref, stk_ref, up_ref)
    outs = (leaf_o, stk_o, up_o)
    share = pl.ds(pl.multiple_of((lax.axis_index("samples") % 4) * 128, 128), 128)
    r = lax.broadcasted_iota(jnp.int32, (128, 128), 0)
    c = lax.broadcasted_iota(jnp.int32, (128, 128), 1)
    lower = r >= c
    scale = math.sqrt(512)
    def blk(b, i):
        return srcs[b][128 * i:128 * i + 128, :]
    def rows(b, i):
        return leaf_ref[128 * i:128 * i + 128, share] if b == 0 else blk(b, i)
    B = range(3)
    for b in B:
        diag[0, b] = mm(blk(b, 0), blk(b, 0), NT)
    g10 = [mm(blk(b, 1), blk(b, 0), NT) for b in B]
    g20 = [mm(blk(b, 2), blk(b, 0), NT) for b in B]
    g11 = [mm(blk(b, 1), blk(b, 1), NT) for b in B]
    g21 = [mm(blk(b, 2), blk(b, 1), NT) for b in B]
    g22 = [mm(blk(b, 2), blk(b, 2), NT) for b in B]
    eliminate(diag.at[0])
    t0 = [jnp.where(lower, diag[0, b], 0.0) for b in B]
    l10 = [mm(g10[b], t0[b], NT) for b in B]
    for b in B:
        diag[1, b] = g11[b] - mm(l10[b], l10[b], NT)
    l20 = [mm(g20[b], t0[b], NT) for b in B]
    g21 = [g21[b] - mm(l20[b], l10[b], NT) for b in B]
    g22 = [g22[b] - mm(l20[b], l20[b], NT) for b in B]
    x0 = [mm(rows(b, 0), t0[b] * scale, TT) for b in B]
    for b in B:
        outs[b][:, :128] = x0[b]
    l10s = [l10[b] * (1 / scale) for b in B]
    l20s = [l20[b] * (1 / scale) for b in B]
    y1 = [rows(b, 1).T - mm(x0[b], l10s[b], NT) for b in B]
    y2 = [rows(b, 2).T - mm(x0[b], l20s[b], NT) for b in B]
    eliminate(diag.at[1])
    t1 = [jnp.where(lower, diag[1, b], 0.0) for b in B]
    l21 = [mm(g21[b], t1[b], NT) for b in B]
    for b in B:
        diag[2, b] = g22[b] - mm(l21[b], l21[b], NT)
    x1 = [mm(y1[b], t1[b] * scale, NT) for b in B]
    for b in B:
        outs[b][:, 128:256] = x1[b]
    y2 = [y2[b] - mm(x1[b], l21[b] * (1 / scale), NT) for b in B]
    eliminate(diag.at[2])
    t2 = [jnp.where(lower, diag[2, b], 0.0) for b in B]
    for b in B:
        outs[b][:, 256:] = mm(y2[b], t2[b] * scale, NT)

def bases(leaf_t, stk_t, up_t):
    vm = pl.BlockSpec(memory_space=pltpu.VMEM)
    f32 = jnp.float32
    return pl.pallas_call(
        factor,
        out_shape=[jax.ShapeDtypeStruct((128, 384), f32), jax.ShapeDtypeStruct((512, 384), f32), jax.ShapeDtypeStruct((512, 384), f32)],
        in_specs=[vm] * 3, out_specs=[vm] * 3,
        scratch_shapes=[pltpu.VMEM((3, 3, 128, 128), f32)],
        compiler_params=pltpu.CompilerParams(vmem_limit_bytes=48 << 20),
        name="bases",
    )(leaf_t, stk_t, up_t)


MESH = pl.DeviceIdType.MESH
SHARE = 48
HALF = 192
PART = 24


def listed(indices, count):
    rows = lax.broadcasted_iota(jnp.int32, (count, indices.shape[1]), 0)
    return jnp.where(rows == indices, 1.0, 0.0).astype(jnp.bfloat16)


def pick_by(values, chosen):
    high = values.astype(jnp.bfloat16)
    rest = values - high.astype(jnp.float32)
    middle = rest.astype(jnp.bfloat16)
    low = (rest - middle.astype(jnp.float32)).astype(jnp.bfloat16)
    found = jnp.dot(jnp.concatenate([high, middle, low], 0), chosen, preferred_element_type=jnp.float32)
    count = values.shape[0]
    return found[:count] + found[count:2 * count] + found[2 * count:]


def pick(values, indices):
    return pick_by(values, listed(indices, values.shape[1]))


def exchange(matrix_ref, sketch_ref, piv_ref, node_ref, leaf_ref, stk_ref, up_ref,
             matrix, sketch, pt_ref, early, swap0, sum0, passing0, parts0, load,
             swap, half_sum, passing, parts, own, own_stk, below, climb_in, climb_out, ring_in, composed, height3, column_in,
             swap_send, swap_recv, pass_send, pass_recv, part_send, part_recv, direct_send, direct_recv,
             relay_send, relay_recv, pair_send, pair_recv, tree_send, tree_recv, ring_recv, column_recv):
    r = lax.axis_index("rows")
    s = lax.axis_index("samples")
    x = s // 2
    c = s % 2
    twin = s + 1 - 2 * c
    beside = (((x + 1) % 4) * 2 + c, ((x + 3) % 4) * 2 + c)
    odd = (r % 2) == 1
    even = jnp.logical_not(odd)
    level2 = (r % 4) == 2
    helper = (r % 8) == 0
    level4 = (r % 16) == 8
    root = (r % 16) == 0

    def load_copy(i):
        if i == 4:
            return pltpu.make_async_copy(sketch_ref, sketch, load.at[4])
        part = pl.ds(256 * i, 256)
        return pltpu.make_async_copy(matrix_ref.at[part, :], matrix.at[part, :], load.at[i])

    for i in (4, 0, 1, 2, 3):
        load_copy(i).start()

    barrier = pltpu.get_barrier_semaphore()

    def greet(row, sample):
        pl.semaphore_signal(barrier, inc=1, device_id=(row, sample), device_id_type=MESH)

    def send(src, dst, sems, to):
        return pltpu.make_async_remote_copy(
            src_ref=src, dst_ref=dst, send_sem=sems[0], recv_sem=sems[1], device_id=to, device_id_type=MESH)

    greet(r, twin)
    greet(r, beside[0])
    greet(r, beside[1])

    @pl.when(odd)
    def _():
        greet(r - 1, s)

    @pl.when(jnp.logical_and(even, jnp.logical_not(helper)))
    def _():
        greet(jnp.where(level2, r - 1, r - 2), s)
        greet(jnp.where(level2, r + 1, r + 2), s)

    @pl.when(helper)
    def _():
        for z in range(1, 8):
            greet(r + z, s)

    @pl.when(level4)
    def _():
        greet(r - 8, s)

    @pl.when(root)
    def _():
        for y in range(1, 4):
            greet((r + 8 * y) % 32, s)

    again = listed(piv_ref[0, 2:3, :], 512)
    handed = [
        jnp.dot(listed(piv_ref[0, h:h + 1, :], 512), again[256 * h:256 * h + 256],
                preferred_element_type=jnp.float32).astype(jnp.bfloat16)
        for h in range(2)
    ]
    load_copy(4).wait()
    for i in range(4):
        load_copy(i).wait()
        product = jnp.dot(matrix[256 * i:256 * i + 256, :], sketch[...], preferred_element_type=jnp.float32)
        pt_ref[:, 256 * i:256 * i + 256] = product.T
    early[...] = pick_by(pt_ref[:, :512], handed[0]) + pick_by(pt_ref[:, 512:], handed[1])

    pl.semaphore_wait(barrier, 5 + jnp.where(level2, 1, 0) + jnp.where(helper, 1, 0))

    def swap_copy(h):
        return send(
            pt_ref.at[pl.ds(pl.multiple_of(HALF * (1 - c), 8), HALF), pl.ds(512 * h, 512)], swap.at[h],
            (swap_send.at[h], swap_recv.at[h]), (r, twin))

    def swap_early():
        return send(
            early.at[pl.ds(pl.multiple_of(HALF * (1 - c), 8), HALF), :], swap0,
            (swap_send.at[2], swap_recv.at[2]), (r, twin))

    swap_early().start()
    swap_copy(0).start()
    swap_copy(1).start()
    group = r // 8

    @pl.when(helper)
    def _():
        top = listed(node_ref[pl.ds(2 + group, 1), :], 512)
        for q in range(2):
            middle = jnp.dot(listed(node_ref[pl.ds(6 + 2 * group + q, 1), :], 512), top[256 * q:256 * q + 256],
                             preferred_element_type=jnp.float32).astype(jnp.bfloat16)
            for p in range(2):
                lower = listed(node_ref[pl.ds(14 + 4 * group + 2 * q + p, 1), :], 512)
                composed[512 * (2 * q + p):512 * (2 * q + p) + 512, :] = jnp.dot(
                    lower, middle[256 * p:256 * p + 256], preferred_element_type=jnp.float32).astype(jnp.bfloat16)

    def share(d, first=0, count=SHARE):
        return pl.ds(pl.multiple_of(SHARE * ((x + d) % 4) + first, 8), count)

    def pass_copy(h, way):
        return send(
            half_sum.at[h, share(2, PART * way, PART), :], passing.at[h, way],
            (pass_send.at[h, way], pass_recv.at[h, way]), (r, beside[way]))

    def part_copy(h, way):
        return send(
            half_sum.at[h, share((1, 3)[way]), :], parts.at[h, way],
            (part_send.at[h, way], part_recv.at[h, way]), (r, beside[way]))

    def pass_early(way):
        return send(
            sum0.at[share(2, PART * way, PART), :], passing0.at[way],
            (pass_send.at[2, way], pass_recv.at[2, way]), (r, beside[way]))

    def part_early(way):
        return send(
            sum0.at[share((1, 3)[way]), :], parts0.at[way],
            (part_send.at[2, way], part_recv.at[2, way]), (r, beside[way]))

    swap_early().wait_recv()
    sum0[...] = early[pl.ds(pl.multiple_of(HALF * c, 8), HALF), :] + swap0[...]
    for way in range(2):
        pass_early(way).start()
    def pass_main(h):
        swap_copy(h).wait_recv()
        half_sum[h] = pt_ref[pl.ds(pl.multiple_of(HALF * c, 8), HALF), 512 * h:512 * h + 512] + swap[h]
        for way in range(2):
            pass_copy(h, way).start()

    pass_main(0)
    for way in range(2):
        pass_early(way).wait_recv()
        sum0[share((1, 3)[way], PART * way, PART), :] += passing0[way]
        part_early(way).start()
    pass_main(1)
    for way in range(2):
        part_early(way).wait_recv()
    skeleton = sum0[share(0), :] + parts0[0] + parts0[1]

    def skeleton_copy():
        return send(below, climb_in.at[:, pl.ds(0, 256)], (tree_send.at[0], tree_recv.at[0]), (r + 1, s))

    def ring_copy():
        return send(
            below, ring_in.at[:, pl.ds(pl.multiple_of(256 * (r % 8), 128), 256)],
            (tree_send.at[2], ring_recv.at[r % 8]), (r - r % 8, s))

    below[...] = skeleton

    @pl.when(helper)
    def _():
        ring_in[:, :256] = skeleton

    @pl.when(jnp.logical_not(helper))
    def _():
        ring_copy().start()

    @pl.when(odd)
    def _():
        climb_in[:, 256:] = skeleton

    @pl.when(even)
    def _():
        skeleton_copy().start()

    for h in range(2):
        for way in range(2):
            pass_copy(h, way).wait_recv()
            mine = share((1, 3)[way], PART * way, PART)
            half_sum[h, mine, :] += passing[h, way]
            part_copy(h, way).start()

    def place(d, first=0, count=SHARE):
        return pl.ds(pl.multiple_of(HALF * c + SHARE * ((x + d) % 4) + first, 8), count)

    outs = (leaf_ref, stk_ref, up_ref)
    OFFSET = (1, 3)

    def direct_copy(n, way, part):
        if n == 0:
            src, dst = own.at[((x + OFFSET[way]) % 4) // 2], leaf_ref.at[place(0), :]
        else:
            first = PART * (way if part == 0 else 1 - way)
            src = (own_stk, climb_in)[n - 1].at[pl.ds(first, PART), :]
            dst = outs[n].at[place(0, first, PART), :]
        return send(src, dst, (direct_send.at[n, way, part], direct_recv.at[n, way, part]), (r, beside[way]))

    def relay_copy(n, way):
        back = OFFSET[1 - way]
        region = outs[n].at[place(back, PART * way, PART), :]
        return send(region, region, (relay_send.at[n, way], relay_recv.at[n, way]), (r, beside[way]))

    first_of_pair = (x % 2) == 0
    mate = jnp.where(first_of_pair, beside[0], beside[1])

    def leaf_relay():
        region = leaf_ref.at[place(jnp.where(first_of_pair, 3, 1)), :]
        return send(region, region, (relay_send.at[0, 0], relay_recv.at[0, 0]), (r, mate))

    def pair_copy(n, d):
        region = outs[n].at[place(d), :]
        return send(region, region, (pair_send.at[n, d], pair_recv.at[n, d]), (r, twin))

    def spread(n):
        for part in range(1 if n == 0 else 2):
            for way in range(2):
                direct_copy(n, way, part).start()
        pair_copy(n, 0).start()

    def collect(n):
        for way in range(2):
            direct_copy(n, way, 0).wait_recv()
            if n > 0:
                relay_copy(n, way).start()
        if n == 0:
            leaf_relay().start()
        for way in range(2):
            if n > 0:
                direct_copy(n, way, 1).wait_recv()
            pair_copy(n, OFFSET[1 - way]).start()

    def finish(n):
        if n == 0:
            leaf_relay().wait_recv()
        else:
            for way in range(2):
                relay_copy(n, way).wait_recv()
        pair_copy(n, 2).start()

    node_row = jnp.where(odd, 14 + r // 2, 6 + r // 4)
    side = jnp.where(odd, (r // 2) % 2, (r // 4) % 2)
    where_to = pl.ds(pl.multiple_of(256 * side, 128), 256)

    def tree_copy(to, sem):
        return send(climb_out, climb_in.at[:, where_to], (tree_send.at[sem], tree_recv.at[side]), (to, s))

    mine_of_four = pl.ds(pl.multiple_of(256 * group, 128), 256)

    def column_copy(which):
        to = jnp.where(r == 0, 16, 0) if which == 0 else jnp.where(root, r + 8, 16)
        return send(
            height3, column_in.at[:, mine_of_four],
            (tree_send.at[1 + 2 * which], column_recv.at[group]), (to, s))

    def arrived(half):
        send(climb_out, climb_in.at[:, pl.ds(256 * half, 256)],
             (tree_send.at[1], tree_recv.at[half]), (r, twin)).wait_recv()

    def column_arrived(y):
        send(height3, column_in.at[:, pl.ds(pl.multiple_of(256 * y, 128), 256)],
             (tree_send.at[1], column_recv.at[y]), (r, twin)).wait_recv()

    def select():
        climb_out[...] = pick(climb_in[...], node_ref[pl.ds(node_row, 1), :])

    up_one = jnp.where(side == 0, r + 1, r - 1)
    up_two = jnp.where(side == 0, r + 2, r - 2)

    @pl.when(odd)
    def _():
        arrived(0)
        select()
        tree_copy(up_one, 1).start()

    for h in range(2):
        for way in range(2):
            part_copy(h, way).wait_recv()
        total = half_sum[h, share(0), :] + parts[h, 0] + parts[h, 1]
        own[h] = total
        own_stk[:, 256 * h:256 * h + 256] = pick(total, piv_ref[0, h:h + 1, :])
    stacked = own_stk[...]
    leaf_ref[place(0), :] = own[x // 2]
    stk_ref[place(0), :] = stacked

    spread(0)
    spread(1)

    @pl.when(level2)
    def _():
        arrived(0)
        arrived(1)
        select()
        tree_copy(up_two, 1).start()

    @pl.when(helper)
    def _():
        for z in range(1, 8):
            send(below, ring_in.at[:, pl.ds(256 * z, 256)],
                 (tree_send.at[2], ring_recv.at[z]), (r, twin)).wait_recv()
        found = pick_by(ring_in[...], composed[...])
        height3[...] = found
        column_in[:, mine_of_four] = found
        for which in range(2):
            column_copy(which).start()

    collect(0)
    collect(1)

    later = jnp.logical_or(odd, jnp.logical_or(level2, helper))

    @pl.when(jnp.logical_not(later))
    def _():
        finish(0)
        finish(1)

    @pl.when(level4)
    def _():
        column_arrived(group - 1)
        climb_in[...] = column_in[:, pl.ds(pl.multiple_of(512 * (group // 2), 128), 512)]

    @pl.when(root)
    def _():
        for y in range(1, 4):
            column_arrived((group + y) % 4)
        for j in range(2):
            climb_in[:, 256 * j:256 * j + 256] = pick(column_in[:, 512 * j:512 * j + 512], node_ref[j:j + 1, :])

    @pl.when((r % 8) == 4)
    def _():
        arrived(0)
        arrived(1)

    up_ref[place(0), :] = climb_in[...]
    spread(2)

    @pl.when(later)
    def _():
        finish(0)
        finish(1)

    collect(2)
    finish(2)

    swap_early().wait_send()
    for way in range(2):
        pass_early(way).wait_send()
        part_early(way).wait_send()
    for h in range(2):
        swap_copy(h).wait_send()
        for way in range(2):
            pass_copy(h, way).wait_send()
            part_copy(h, way).wait_send()

    @pl.when(even)
    def _():
        skeleton_copy().wait_send()

    @pl.when(odd)
    def _():
        tree_copy(up_one, 1).wait_send()

    @pl.when(level2)
    def _():
        tree_copy(up_two, 1).wait_send()

    @pl.when(helper)
    def _():
        for which in range(2):
            column_copy(which).wait_send()

    @pl.when(jnp.logical_not(helper))
    def _():
        ring_copy().wait_send()

    leaf_relay().wait_send()
    for n in range(3):
        for way in range(2):
            direct_copy(n, way, 0).wait_send()
            if n > 0:
                direct_copy(n, way, 1).wait_send()
                relay_copy(n, way).wait_send()
        for d in range(4):
            pair_copy(n, d).wait()


def gathered(matrix, sketch, pivots, node_pivots):
    vmem = pl.BlockSpec(memory_space=pltpu.VMEM)
    f32 = jnp.float32
    dma = pltpu.SemaphoreType.DMA
    return pl.pallas_call(
        exchange,
        out_shape=[jax.ShapeDtypeStruct((384, 512), f32)] * 3,
        in_specs=[pl.BlockSpec(memory_space=pltpu.MemorySpace.HBM)] * 2 + [vmem] * 2, out_specs=[vmem] * 3,
        scratch_shapes=[
            pltpu.VMEM(matrix.shape, matrix.dtype), pltpu.VMEM(sketch.shape, sketch.dtype),
            pltpu.VMEM((384, 1024), f32), pltpu.VMEM((384, 256), f32), pltpu.VMEM((HALF, 256), f32), pltpu.VMEM((HALF, 256), f32),
            pltpu.VMEM((2, PART, 256), f32), pltpu.VMEM((2, SHARE, 256), f32), dma((5,)),
            pltpu.VMEM((2, HALF, 512), f32), pltpu.VMEM((2, HALF, 512), f32),
            pltpu.VMEM((2, 2, PART, 512), f32), pltpu.VMEM((2, 2, SHARE, 512), f32),
            pltpu.VMEM((2, SHARE, 512), f32), pltpu.VMEM((SHARE, 512), f32), pltpu.VMEM((SHARE, 256), f32),
            pltpu.VMEM((SHARE, 512), f32), pltpu.VMEM((SHARE, 256), f32),
            pltpu.VMEM((SHARE, 2048), f32), pltpu.VMEM((2048, 256), jnp.bfloat16),
            pltpu.VMEM((SHARE, 256), f32), pltpu.VMEM((SHARE, 1024), f32),
            dma((3,)), dma((3,)), dma((3, 2)), dma((3, 2)), dma((3, 2)), dma((3, 2)), dma((3, 2, 2)), dma((3, 2, 2)),
            dma((3, 2)), dma((3, 2)), dma((3, 4)), dma((3, 4)), dma((4,)), dma((2,)), dma((8,)), dma((4,)),
        ],
        compiler_params=pltpu.CompilerParams(collective_id=0, has_side_effects=True, vmem_limit_bytes=48 << 20),
        name="exchange",
    )(matrix, sketch, pivots, node_pivots)


def on_device(matrix_block, sketch_matrix, local_pivots, upper_pivots):
    return tuple(bases(*gathered(matrix_block, sketch_matrix, local_pivots, upper_pivots)))


def solution(mesh):
    in_specs = (P("rows", "samples"), P("samples", None), P("rows", None, None), P())
    out_specs = (P(("rows", "samples"), None), P("rows", None), P("rows", None))
    return jax.shard_map(
        on_device, mesh=mesh, in_specs=in_specs, out_specs=out_specs, check_vma=False
    )
```

```python
import math

import jax
import jax.numpy as jnp
from jax import lax
from jax.experimental import pallas as pl
from jax.experimental.pallas import tpu as pltpu
from jax.sharding import PartitionSpec as P

SUBS = 4
NN = (((1,), (0,)), ((), ()))
NT = (((1,), (1,)), ((), ()))
TN = (((0,), (0,)), ((), ()))
TT = (((0,), (1,)), ((), ()))

def mm(a, b, dims):
    return lax.dot_general(a, b, dims, precision=lax.Precision.HIGH, preferred_element_type=jnp.float32)

def row_of(x, i):
    return jnp.broadcast_to(x[:, i:i + 1, :], x.shape)

def eliminate(m_ref):
    batch = m_ref.shape[0]
    shape = (batch, 8, 128)
    sub = lax.broadcasted_iota(jnp.int32, shape, 1)
    lane = lax.broadcasted_iota(jnp.int32, shape, 2)
    span = 8 * SUBS
    for start in range(0, 128, span):
        groups = [m_ref[:, start + 8 * g:start + 8 * g + 8, :] for g in range(SUBS)]
        for q in range(SUBS):
            lo = start + 8 * q
            in_block = (lane >= lo) & (lane < lo + 8)
            cols = [None] * q + [[jnp.broadcast_to(groups[g][:, :, lo + j:lo + j + 1], shape) for j in range(8)] for g in range(q, SUBS)]
            groups[q] = jnp.where(in_block, jnp.where(lane - lo == sub, 1.0, 0.0), groups[q])
            for g in range(q + 1, SUBS):
                groups[g] = jnp.where(in_block, 0.0, groups[g])
            pivot = row_of(cols[q][0], 0)
            for j in range(8):
                scale = lax.rsqrt(pivot)
                inverse = scale * scale
                own = cols[q]
                column = own[j]
                if j < 7:
                    raw = row_of(column, j + 1)
                    pivot = row_of(own[j + 1], j + 1) - (raw * raw) * inverse
                for i in range(j + 1, 8):
                    factor = row_of(column, i) * inverse
                    for g in range(q, SUBS):
                        cols[g][i] = cols[g][i] - cols[g][j] * factor
                base = row_of(groups[q], j)
                scaled = base * inverse
                groups[q] = jnp.where(sub == j, base * scale, groups[q] - jnp.where(sub > j, column, 0.0) * scaled)
                for g in range(q + 1, SUBS):
                    groups[g] = groups[g] - cols[g][j] * scaled
        for g in range(SUBS):
            m_ref[:, start + 8 * g:start + 8 * g + 8, :] = groups[g]
        rest = start + span
        if rest < 128:
            for b in range(batch):
                panel = jnp.concatenate([groups[g][b] for g in range(SUBS)], 0)
                prow = lax.broadcasted_iota(jnp.int32, panel.shape, 0)
                plane = lax.broadcasted_iota(jnp.int32, panel.shape, 1)
                done = jnp.where((plane >= start) & (plane < rest) & (plane - start >= (prow // 8) * 8 + 8), 0.0, panel)
                upd = mm(panel.T[rest:], done, NN)
                keep = m_ref[b, rest:, :]
                lane2 = lax.broadcasted_iota(jnp.int32, keep.shape, 1)
                keep = jnp.where((lane2 >= start) & (lane2 < rest), 0.0, keep)
                m_ref[b, rest:, :] = keep - upd


def factor(leaf_ref, stk_ref, up_ref, leaf_o, stk_o, up_o, diag):
    srcs = (leaf_ref, stk_ref, up_ref)
    outs = (leaf_o, stk_o, up_o)
    share = pl.ds(pl.multiple_of((lax.axis_index("samples") % 4) * 128, 128), 128)
    r = lax.broadcasted_iota(jnp.int32, (128, 128), 0)
    c = lax.broadcasted_iota(jnp.int32, (128, 128), 1)
    lower = r >= c
    scale = math.sqrt(512)
    def blk(b, i):
        return srcs[b][128 * i:128 * i + 128, :]
    def rows(b, i):
        return leaf_ref[128 * i:128 * i + 128, share] if b == 0 else blk(b, i)
    B = range(3)
    for b in B:
        diag[0, b] = mm(blk(b, 0), blk(b, 0), NT)
    g10 = [mm(blk(b, 1), blk(b, 0), NT) for b in B]
    g20 = [mm(blk(b, 2), blk(b, 0), NT) for b in B]
    g11 = [mm(blk(b, 1), blk(b, 1), NT) for b in B]
    g21 = [mm(blk(b, 2), blk(b, 1), NT) for b in B]
    g22 = [mm(blk(b, 2), blk(b, 2), NT) for b in B]
    eliminate(diag.at[0])
    t0 = [jnp.where(lower, diag[0, b], 0.0) for b in B]
    l10 = [mm(g10[b], t0[b], NT) for b in B]
    for b in B:
        diag[1, b] = g11[b] - mm(l10[b], l10[b], NT)
    l20 = [mm(g20[b], t0[b], NT) for b in B]
    g21 = [g21[b] - mm(l20[b], l10[b], NT) for b in B]
    g22 = [g22[b] - mm(l20[b], l20[b], NT) for b in B]
    x0 = [mm(rows(b, 0), t0[b] * scale, TT) for b in B]
    for b in B:
        outs[b][:, :128] = x0[b]
    l10s = [l10[b] * (1 / scale) for b in B]
    l20s = [l20[b] * (1 / scale) for b in B]
    y1 = [rows(b, 1).T - mm(x0[b], l10s[b], NT) for b in B]
    y2 = [rows(b, 2).T - mm(x0[b], l20s[b], NT) for b in B]
    eliminate(diag.at[1])
    t1 = [jnp.where(lower, diag[1, b], 0.0) for b in B]
    l21 = [mm(g21[b], t1[b], NT) for b in B]
    for b in B:
        diag[2, b] = g22[b] - mm(l21[b], l21[b], NT)
    x1 = [mm(y1[b], t1[b] * scale, NT) for b in B]
    for b in B:
        outs[b][:, 128:256] = x1[b]
    y2 = [y2[b] - mm(x1[b], l21[b] * (1 / scale), NT) for b in B]
    eliminate(diag.at[2])
    t2 = [jnp.where(lower, diag[2, b], 0.0) for b in B]
    for b in B:
        outs[b][:, 256:] = mm(y2[b], t2[b] * scale, NT)

def bases(leaf_t, stk_t, up_t):
    vm = pl.BlockSpec(memory_space=pltpu.VMEM)
    f32 = jnp.float32
    return pl.pallas_call(
        factor,
        out_shape=[jax.ShapeDtypeStruct((128, 384), f32), jax.ShapeDtypeStruct((512, 384), f32), jax.ShapeDtypeStruct((512, 384), f32)],
        in_specs=[vm] * 3, out_specs=[vm] * 3,
        scratch_shapes=[pltpu.VMEM((3, 3, 128, 128), f32)],
        compiler_params=pltpu.CompilerParams(vmem_limit_bytes=48 << 20),
        name="bases",
    )(leaf_t, stk_t, up_t)


MESH = pl.DeviceIdType.MESH
SHARE = 48
HALF = 192
PART = 24


def listed(indices, count):
    rows = lax.broadcasted_iota(jnp.int32, (count, indices.shape[1]), 0)
    return jnp.where(rows == indices, 1.0, 0.0).astype(jnp.bfloat16)


def pick_by(values, chosen):
    high = values.astype(jnp.bfloat16)
    rest = values - high.astype(jnp.float32)
    middle = rest.astype(jnp.bfloat16)
    low = (rest - middle.astype(jnp.float32)).astype(jnp.bfloat16)
    found = jnp.dot(jnp.concatenate([high, middle, low], 0), chosen, preferred_element_type=jnp.float32)
    count = values.shape[0]
    return found[:count] + found[count:2 * count] + found[2 * count:]


def pick(values, indices):
    return pick_by(values, listed(indices, values.shape[1]))


def exchange(matrix_ref, sketch_ref, piv_ref, node_ref, leaf_ref, stk_ref, up_ref,
             matrix, sketch, pt_ref, early, swap0, sum0, passing0, parts0, load,
             swap, half_sum, passing, parts, own, own_stk, below, climb_in, climb_out, ring_in, composed, height3, column_in,
             swap_send, swap_recv, pass_send, pass_recv, part_send, part_recv, direct_send, direct_recv,
             relay_send, relay_recv, pair_send, pair_recv, tree_send, tree_recv, ring_recv, column_recv):
    r = lax.axis_index("rows")
    s = lax.axis_index("samples")
    x = s // 2
    c = s % 2
    twin = s + 1 - 2 * c
    beside = (((x + 1) % 4) * 2 + c, ((x + 3) % 4) * 2 + c)
    odd = (r % 2) == 1
    even = jnp.logical_not(odd)
    level2 = (r % 4) == 2
    helper = (r % 8) == 0
    level4 = (r % 16) == 8
    root = (r % 16) == 0

    def load_copy(i):
        if i == 4:
            return pltpu.make_async_copy(sketch_ref, sketch, load.at[4])
        part = pl.ds(256 * i, 256)
        return pltpu.make_async_copy(matrix_ref.at[part, :], matrix.at[part, :], load.at[i])

    for i in (4, 0, 1, 2, 3):
        load_copy(i).start()

    barrier = pltpu.get_barrier_semaphore()

    def greet(row, sample):
        pl.semaphore_signal(barrier, inc=1, device_id=(row, sample), device_id_type=MESH)

    def send(src, dst, sems, to):
        return pltpu.make_async_remote_copy(
            src_ref=src, dst_ref=dst, send_sem=sems[0], recv_sem=sems[1], device_id=to, device_id_type=MESH)

    greet(r, twin)
    greet(r, beside[0])
    greet(r, beside[1])

    @pl.when(odd)
    def _():
        greet(r - 1, s)

    @pl.when(jnp.logical_and(even, jnp.logical_not(helper)))
    def _():
        greet(jnp.where(level2, r - 1, r - 2), s)
        greet(jnp.where(level2, r + 1, r + 2), s)

    @pl.when(helper)
    def _():
        for z in range(1, 8):
            greet(r + z, s)

    @pl.when(level4)
    def _():
        greet(r - 8, s)

    @pl.when(root)
    def _():
        for y in range(1, 4):
            greet((r + 8 * y) % 32, s)

    again = listed(piv_ref[0, 2:3, :], 512)
    handed = [
        jnp.dot(listed(piv_ref[0, h:h + 1, :], 512), again[256 * h:256 * h + 256],
                preferred_element_type=jnp.float32).astype(jnp.bfloat16)
        for h in range(2)
    ]
    load_copy(4).wait()
    for i in range(4):
        load_copy(i).wait()
        product = jnp.dot(matrix[256 * i:256 * i + 256, :], sketch[...], preferred_element_type=jnp.float32)
        pt_ref[:, 256 * i:256 * i + 256] = product.T
    early[...] = pick_by(pt_ref[:, :512], handed[0]) + pick_by(pt_ref[:, 512:], handed[1])

    pl.semaphore_wait(barrier, 5 + jnp.where(level2, 1, 0) + jnp.where(helper, 1, 0))

    def swap_copy(h):
        return send(
            pt_ref.at[pl.ds(pl.multiple_of(HALF * (1 - c), 8), HALF), pl.ds(512 * h, 512)], swap.at[h],
            (swap_send.at[h], swap_recv.at[h]), (r, twin))

    def swap_early():
        return send(
            early.at[pl.ds(pl.multiple_of(HALF * (1 - c), 8), HALF), :], swap0,
            (swap_send.at[2], swap_recv.at[2]), (r, twin))

    swap_early().start()
    swap_copy(0).start()
    swap_copy(1).start()
    group = r // 8

    @pl.when(helper)
    def _():
        top = listed(node_ref[pl.ds(2 + group, 1), :], 512)
        for q in range(2):
            middle = jnp.dot(listed(node_ref[pl.ds(6 + 2 * group + q, 1), :], 512), top[256 * q:256 * q + 256],
                             preferred_element_type=jnp.float32).astype(jnp.bfloat16)
            for p in range(2):
                lower = listed(node_ref[pl.ds(14 + 4 * group + 2 * q + p, 1), :], 512)
                composed[512 * (2 * q + p):512 * (2 * q + p) + 512, :] = jnp.dot(
                    lower, middle[256 * p:256 * p + 256], preferred_element_type=jnp.float32).astype(jnp.bfloat16)

    def share(d, first=0, count=SHARE):
        return pl.ds(pl.multiple_of(SHARE * ((x + d) % 4) + first, 8), count)

    def pass_copy(h, way):
        return send(
            half_sum.at[h, share(2, PART * way, PART), :], passing.at[h, way],
            (pass_send.at[h, way], pass_recv.at[h, way]), (r, beside[way]))

    def part_copy(h, way):
        return send(
            half_sum.at[h, share((1, 3)[way]), :], parts.at[h, way],
            (part_send.at[h, way], part_recv.at[h, way]), (r, beside[way]))

    def pass_early(way):
        return send(
            sum0.at[share(2, PART * way, PART), :], passing0.at[way],
            (pass_send.at[2, way], pass_recv.at[2, way]), (r, beside[way]))

    def part_early(way):
        return send(
            sum0.at[share((1, 3)[way]), :], parts0.at[way],
            (part_send.at[2, way], part_recv.at[2, way]), (r, beside[way]))

    swap_early().wait_recv()
    sum0[...] = early[pl.ds(pl.multiple_of(HALF * c, 8), HALF), :] + swap0[...]
    for way in range(2):
        pass_early(way).start()
    def pass_main(h):
        swap_copy(h).wait_recv()
        half_sum[h] = pt_ref[pl.ds(pl.multiple_of(HALF * c, 8), HALF), 512 * h:512 * h + 512] + swap[h]
        for way in range(2):
            pass_copy(h, way).start()

    pass_main(0)
    for way in range(2):
        pass_early(way).wait_recv()
        sum0[share((1, 3)[way], PART * way, PART), :] += passing0[way]
        part_early(way).start()
    pass_main(1)
    for way in range(2):
        part_early(way).wait_recv()
    skeleton = sum0[share(0), :] + parts0[0] + parts0[1]

    def skeleton_copy():
        return send(below, climb_in.at[:, pl.ds(0, 256)], (tree_send.at[0], tree_recv.at[0]), (r + 1, s))

    def ring_copy():
        return send(
            below, ring_in.at[:, pl.ds(pl.multiple_of(256 * (r % 8), 128), 256)],
            (tree_send.at[2], ring_recv.at[r % 8]), (r - r % 8, s))

    below[...] = skeleton

    @pl.when(helper)
    def _():
        ring_in[:, :256] = skeleton

    @pl.when(jnp.logical_not(helper))
    def _():
        ring_copy().start()

    @pl.when(odd)
    def _():
        climb_in[:, 256:] = skeleton

    @pl.when(even)
    def _():
        skeleton_copy().start()

    for h in range(2):
        for way in range(2):
            pass_copy(h, way).wait_recv()
            mine = share((1, 3)[way], PART * way, PART)
            half_sum[h, mine, :] += passing[h, way]
            part_copy(h, way).start()

    def place(d, first=0, count=SHARE):
        return pl.ds(pl.multiple_of(HALF * c + SHARE * ((x + d) % 4) + first, 8), count)

    outs = (leaf_ref, stk_ref, up_ref)
    OFFSET = (1, 3)

    def direct_copy(n, way, part):
        if n == 0:
            src, dst = own.at[((x + OFFSET[way]) % 4) // 2], leaf_ref.at[place(0), :]
        else:
            first = PART * (way if part == 0 else 1 - way)
            src = (own_stk, climb_in)[n - 1].at[pl.ds(first, PART), :]
            dst = outs[n].at[place(0, first, PART), :]
        return send(src, dst, (direct_send.at[n, way, part], direct_recv.at[n, way, part]), (r, beside[way]))

    def relay_copy(n, way):
        back = OFFSET[1 - way]
        region = outs[n].at[place(back, PART * way, PART), :]
        return send(region, region, (relay_send.at[n, way], relay_recv.at[n, way]), (r, beside[way]))

    first_of_pair = (x % 2) == 0
    mate = jnp.where(first_of_pair, beside[0], beside[1])

    def leaf_relay():
        region = leaf_ref.at[place(jnp.where(first_of_pair, 3, 1)), :]
        return send(region, region, (relay_send.at[0, 0], relay_recv.at[0, 0]), (r, mate))

    def pair_copy(n, d):
        region = outs[n].at[place(d), :]
        return send(region, region, (pair_send.at[n, d], pair_recv.at[n, d]), (r, twin))

    def spread(n):
        for part in range(1 if n == 0 else 2):
            for way in range(2):
                direct_copy(n, way, part).start()
        pair_copy(n, 0).start()

    def collect(n):
        for way in range(2):
            direct_copy(n, way, 0).wait_recv()
            if n > 0:
                relay_copy(n, way).start()
        if n == 0:
            leaf_relay().start()
        for way in range(2):
            if n > 0:
                direct_copy(n, way, 1).wait_recv()
            pair_copy(n, OFFSET[1 - way]).start()

    def finish(n):
        if n == 0:
            leaf_relay().wait_recv()
        else:
            for way in range(2):
                relay_copy(n, way).wait_recv()
        pair_copy(n, 2).start()

    node_row = jnp.where(odd, 14 + r // 2, 6 + r // 4)
    side = jnp.where(odd, (r // 2) % 2, (r // 4) % 2)
    where_to = pl.ds(pl.multiple_of(256 * side, 128), 256)

    def tree_copy(to, sem):
        return send(climb_out, climb_in.at[:, where_to], (tree_send.at[sem], tree_recv.at[side]), (to, s))

    mine_of_four = pl.ds(pl.multiple_of(256 * group, 128), 256)

    def column_copy(which):
        to = jnp.where(r == 0, 16, 0) if which == 0 else jnp.where(root, r + 8, 16)
        return send(
            height3, column_in.at[:, mine_of_four],
            (tree_send.at[1 + 2 * which], column_recv.at[group]), (to, s))

    def arrived(half):
        send(climb_out, climb_in.at[:, pl.ds(256 * half, 256)],
             (tree_send.at[1], tree_recv.at[half]), (r, twin)).wait_recv()

    def column_arrived(y):
        send(height3, column_in.at[:, pl.ds(pl.multiple_of(256 * y, 128), 256)],
             (tree_send.at[1], column_recv.at[y]), (r, twin)).wait_recv()

    def select():
        climb_out[...] = pick(climb_in[...], node_ref[pl.ds(node_row, 1), :])

    up_one = jnp.where(side == 0, r + 1, r - 1)
    up_two = jnp.where(side == 0, r + 2, r - 2)

    @pl.when(odd)
    def _():
        arrived(0)
        select()
        tree_copy(up_one, 1).start()

    for h in range(2):
        for way in range(2):
            part_copy(h, way).wait_recv()
        total = half_sum[h, share(0), :] + parts[h, 0] + parts[h, 1]
        own[h] = total
        own_stk[:, 256 * h:256 * h + 256] = pick(total, piv_ref[0, h:h + 1, :])
    stacked = own_stk[...]
    leaf_ref[place(0), :] = own[x // 2]
    stk_ref[place(0), :] = stacked

    spread(0)
    spread(1)

    @pl.when(level2)
    def _():
        arrived(0)
        arrived(1)
        select()
        tree_copy(up_two, 1).start()

    @pl.when(helper)
    def _():
        for z in range(1, 8):
            send(below, ring_in.at[:, pl.ds(256 * z, 256)],
                 (tree_send.at[2], ring_recv.at[z]), (r, twin)).wait_recv()
        found = pick_by(ring_in[...], composed[...])
        height3[...] = found
        column_in[:, mine_of_four] = found
        for which in range(2):
            column_copy(which).start()

    collect(0)
    collect(1)

    later = jnp.logical_or(odd, jnp.logical_or(level2, helper))

    @pl.when(jnp.logical_not(later))
    def _():
        finish(0)
        finish(1)

    @pl.when(level4)
    def _():
        column_arrived(group - 1)
        climb_in[...] = column_in[:, pl.ds(pl.multiple_of(512 * (group // 2), 128), 512)]

    @pl.when(root)
    def _():
        for y in range(1, 4):
            column_arrived((group + y) % 4)
        for j in range(2):
            climb_in[:, 256 * j:256 * j + 256] = pick(column_in[:, 512 * j:512 * j + 512], node_ref[j:j + 1, :])

    @pl.when((r % 8) == 4)
    def _():
        arrived(0)
        arrived(1)

    up_ref[place(0), :] = climb_in[...]
    spread(2)

    @pl.when(later)
    def _():
        finish(0)
        finish(1)

    collect(2)
    finish(2)

    swap_early().wait_send()
    for way in range(2):
        pass_early(way).wait_send()
        part_early(way).wait_send()
    for h in range(2):
        swap_copy(h).wait_send()
        for way in range(2):
            pass_copy(h, way).wait_send()
            part_copy(h, way).wait_send()

    @pl.when(even)
    def _():
        skeleton_copy().wait_send()

    @pl.when(odd)
    def _():
        tree_copy(up_one, 1).wait_send()

    @pl.when(level2)
    def _():
        tree_copy(up_two, 1).wait_send()

    @pl.when(helper)
    def _():
        for which in range(2):
            column_copy(which).wait_send()

    @pl.when(jnp.logical_not(helper))
    def _():
        ring_copy().wait_send()

    leaf_relay().wait_send()
    for n in range(3):
        for way in range(2):
            direct_copy(n, way, 0).wait_send()
            if n > 0:
                direct_copy(n, way, 1).wait_send()
                relay_copy(n, way).wait_send()
        for d in range(4):
            pair_copy(n, d).wait()


def gathered(matrix, sketch, pivots, node_pivots):
    vmem = pl.BlockSpec(memory_space=pltpu.VMEM)
    f32 = jnp.float32
    dma = pltpu.SemaphoreType.DMA
    return pl.pallas_call(
        exchange,
        out_shape=[jax.ShapeDtypeStruct((384, 512), f32)] * 3,
        in_specs=[pl.BlockSpec(memory_space=pltpu.MemorySpace.HBM)] * 2 + [vmem] * 2, out_specs=[vmem] * 3,
        scratch_shapes=[
            pltpu.VMEM(matrix.shape, matrix.dtype), pltpu.VMEM(sketch.shape, sketch.dtype),
            pltpu.VMEM((384, 1024), f32), pltpu.VMEM((384, 256), f32), pltpu.VMEM((HALF, 256), f32), pltpu.VMEM((HALF, 256), f32),
            pltpu.VMEM((2, PART, 256), f32), pltpu.VMEM((2, SHARE, 256), f32), dma((5,)),
            pltpu.VMEM((2, HALF, 512), f32), pltpu.VMEM((2, HALF, 512), f32),
            pltpu.VMEM((2, 2, PART, 512), f32), pltpu.VMEM((2, 2, SHARE, 512), f32),
            pltpu.VMEM((2, SHARE, 512), f32), pltpu.VMEM((SHARE, 512), f32), pltpu.VMEM((SHARE, 256), f32),
            pltpu.VMEM((SHARE, 512), f32), pltpu.VMEM((SHARE, 256), f32),
            pltpu.VMEM((SHARE, 2048), f32), pltpu.VMEM((2048, 256), jnp.bfloat16),
            pltpu.VMEM((SHARE, 256), f32), pltpu.VMEM((SHARE, 1024), f32),
            dma((3,)), dma((3,)), dma((3, 2)), dma((3, 2)), dma((3, 2)), dma((3, 2)), dma((3, 2, 2)), dma((3, 2, 2)),
            dma((3, 2)), dma((3, 2)), dma((3, 4)), dma((3, 4)), dma((4,)), dma((2,)), dma((8,)), dma((4,)),
        ],
        compiler_params=pltpu.CompilerParams(collective_id=0, has_side_effects=True, vmem_limit_bytes=50 << 20),
        name="exchange",
    )(matrix, sketch, pivots, node_pivots)


def on_device(matrix_block, sketch_matrix, local_pivots, upper_pivots):
    return tuple(bases(*gathered(matrix_block, sketch_matrix, local_pivots, upper_pivots)))


def solution(mesh):
    in_specs = (P("rows", "samples"), P("samples", None), P("rows", None, None), P())
    out_specs = (P(("rows", "samples"), None), P("rows", None), P("rows", None))
    return jax.shard_map(
        on_device, mesh=mesh, in_specs=in_specs, out_specs=out_specs, check_vma=False
    )
```

```python
import math

import jax
import jax.numpy as jnp
from jax import lax
from jax.experimental import pallas as pl
from jax.experimental.pallas import tpu as pltpu
from jax.sharding import PartitionSpec as P

SUBS = 4
NN = (((1,), (0,)), ((), ()))
NT = (((1,), (1,)), ((), ()))
TN = (((0,), (0,)), ((), ()))
TT = (((0,), (1,)), ((), ()))

def mm(a, b, dims):
    return lax.dot_general(a, b, dims, precision=lax.Precision.HIGH, preferred_element_type=jnp.float32)

def row_of(x, i):
    return jnp.broadcast_to(x[:, i:i + 1, :], x.shape)

def eliminate(m_ref):
    batch = m_ref.shape[0]
    shape = (batch, 8, 128)
    sub = lax.broadcasted_iota(jnp.int32, shape, 1)
    lane = lax.broadcasted_iota(jnp.int32, shape, 2)
    span = 8 * SUBS
    for start in range(0, 128, span):
        groups = [m_ref[:, start + 8 * g:start + 8 * g + 8, :] for g in range(SUBS)]
        for q in range(SUBS):
            lo = start + 8 * q
            in_block = (lane >= lo) & (lane < lo + 8)
            cols = [None] * q + [[jnp.broadcast_to(groups[g][:, :, lo + j:lo + j + 1], shape) for j in range(8)] for g in range(q, SUBS)]
            groups[q] = jnp.where(in_block, jnp.where(lane - lo == sub, 1.0, 0.0), groups[q])
            for g in range(q + 1, SUBS):
                groups[g] = jnp.where(in_block, 0.0, groups[g])
            pivot = row_of(cols[q][0], 0)
            for j in range(8):
                scale = lax.rsqrt(pivot)
                inverse = scale * scale
                own = cols[q]
                column = own[j]
                if j < 7:
                    raw = row_of(column, j + 1)
                    pivot = row_of(own[j + 1], j + 1) - (raw * raw) * inverse
                for i in range(j + 1, 8):
                    factor = row_of(column, i) * inverse
                    for g in range(q, SUBS):
                        cols[g][i] = cols[g][i] - cols[g][j] * factor
                base = row_of(groups[q], j)
                scaled = base * inverse
                groups[q] = jnp.where(sub == j, base * scale, groups[q] - jnp.where(sub > j, column, 0.0) * scaled)
                for g in range(q + 1, SUBS):
                    groups[g] = groups[g] - cols[g][j] * scaled
        for g in range(SUBS):
            m_ref[:, start + 8 * g:start + 8 * g + 8, :] = groups[g]
        rest = start + span
        if rest < 128:
            for b in range(batch):
                panel = jnp.concatenate([groups[g][b] for g in range(SUBS)], 0)
                prow = lax.broadcasted_iota(jnp.int32, panel.shape, 0)
                plane = lax.broadcasted_iota(jnp.int32, panel.shape, 1)
                done = jnp.where((plane >= start) & (plane < rest) & (plane - start >= (prow // 8) * 8 + 8), 0.0, panel)
                upd = mm(panel.T[rest:], done, NN)
                keep = m_ref[b, rest:, :]
                lane2 = lax.broadcasted_iota(jnp.int32, keep.shape, 1)
                keep = jnp.where((lane2 >= start) & (lane2 < rest), 0.0, keep)
                m_ref[b, rest:, :] = keep - upd


def factor(leaf_ref, stk_ref, up_ref, leaf_o, stk_o, up_o, diag):
    srcs = (leaf_ref, stk_ref, up_ref)
    outs = (leaf_o, stk_o, up_o)
    share = pl.ds(pl.multiple_of((lax.axis_index("samples") % 4) * 128, 128), 128)
    r = lax.broadcasted_iota(jnp.int32, (128, 128), 0)
    c = lax.broadcasted_iota(jnp.int32, (128, 128), 1)
    lower = r >= c
    scale = math.sqrt(512)
    def blk(b, i):
        return srcs[b][128 * i:128 * i + 128, :]
    def rows(b, i):
        return leaf_ref[128 * i:128 * i + 128, share] if b == 0 else blk(b, i)
    B = range(3)
    for b in B:
        diag[0, b] = mm(blk(b, 0), blk(b, 0), NT)
    g10 = [mm(blk(b, 1), blk(b, 0), NT) for b in B]
    g20 = [mm(blk(b, 2), blk(b, 0), NT) for b in B]
    g11 = [mm(blk(b, 1), blk(b, 1), NT) for b in B]
    g21 = [mm(blk(b, 2), blk(b, 1), NT) for b in B]
    g22 = [mm(blk(b, 2), blk(b, 2), NT) for b in B]
    eliminate(diag.at[0])
    t0 = [jnp.where(lower, diag[0, b], 0.0) for b in B]
    l10 = [mm(g10[b], t0[b], NT) for b in B]
    for b in B:
        diag[1, b] = g11[b] - mm(l10[b], l10[b], NT)
    l20 = [mm(g20[b], t0[b], NT) for b in B]
    g21 = [g21[b] - mm(l20[b], l10[b], NT) for b in B]
    g22 = [g22[b] - mm(l20[b], l20[b], NT) for b in B]
    x0 = [mm(rows(b, 0), t0[b] * scale, TT) for b in B]
    for b in B:
        outs[b][:, :128] = x0[b]
    l10s = [l10[b] * (1 / scale) for b in B]
    l20s = [l20[b] * (1 / scale) for b in B]
    y1 = [rows(b, 1).T - mm(x0[b], l10s[b], NT) for b in B]
    y2 = [rows(b, 2).T - mm(x0[b], l20s[b], NT) for b in B]
    eliminate(diag.at[1])
    t1 = [jnp.where(lower, diag[1, b], 0.0) for b in B]
    l21 = [mm(g21[b], t1[b], NT) for b in B]
    for b in B:
        diag[2, b] = g22[b] - mm(l21[b], l21[b], NT)
    x1 = [mm(y1[b], t1[b] * scale, NT) for b in B]
    for b in B:
        outs[b][:, 128:256] = x1[b]
    y2 = [y2[b] - mm(x1[b], l21[b] * (1 / scale), NT) for b in B]
    eliminate(diag.at[2])
    t2 = [jnp.where(lower, diag[2, b], 0.0) for b in B]
    for b in B:
        outs[b][:, 256:] = mm(y2[b], t2[b] * scale, NT)

def bases(leaf_t, stk_t, up_t):
    vm = pl.BlockSpec(memory_space=pltpu.VMEM)
    f32 = jnp.float32
    return pl.pallas_call(
        factor,
        out_shape=[jax.ShapeDtypeStruct((128, 384), f32), jax.ShapeDtypeStruct((512, 384), f32), jax.ShapeDtypeStruct((512, 384), f32)],
        in_specs=[vm] * 3, out_specs=[vm] * 3,
        scratch_shapes=[pltpu.VMEM((3, 3, 128, 128), f32)],
        compiler_params=pltpu.CompilerParams(vmem_limit_bytes=48 << 20),
        name="bases",
    )(leaf_t, stk_t, up_t)


MESH = pl.DeviceIdType.MESH
SHARE = 48
HALF = 192
PART = 24


def listed(indices, count):
    rows = lax.broadcasted_iota(jnp.int32, (count, indices.shape[1]), 0)
    return jnp.where(rows == indices, 1.0, 0.0).astype(jnp.bfloat16)


def pick_by(values, chosen):
    high = values.astype(jnp.bfloat16)
    rest = values - high.astype(jnp.float32)
    middle = rest.astype(jnp.bfloat16)
    low = (rest - middle.astype(jnp.float32)).astype(jnp.bfloat16)
    found = jnp.dot(jnp.concatenate([high, middle, low], 0), chosen, preferred_element_type=jnp.float32)
    count = values.shape[0]
    return found[:count] + found[count:2 * count] + found[2 * count:]


def pick(values, indices):
    return pick_by(values, listed(indices, values.shape[1]))


def exchange(matrix_ref, sketch_ref, piv_ref, node_ref, leaf_ref, stk_ref, up_ref,
             matrix, sketch, pt_ref, early, swap0, sum0, passing0, parts0, load,
             swap, half_sum, passing, parts, own, own_stk, below, climb_in, climb_out, ring_in, composed, height3, column_in,
             swap_send, swap_recv, pass_send, pass_recv, part_send, part_recv, direct_send, direct_recv,
             relay_send, relay_recv, pair_send, pair_recv, tree_send, tree_recv, ring_recv, column_recv, cross_send, cross_recv):
    r = lax.axis_index("rows")
    s = lax.axis_index("samples")
    x = s // 2
    c = s % 2
    twin = s + 1 - 2 * c
    beside = (((x + 1) % 4) * 2 + c, ((x + 3) % 4) * 2 + c)
    across = (((x + 1) % 4) * 2 + 1 - c, ((x + 3) % 4) * 2 + 1 - c)
    odd = (r % 2) == 1
    even = jnp.logical_not(odd)
    level2 = (r % 4) == 2
    helper = (r % 8) == 0
    level4 = (r % 16) == 8
    root = (r % 16) == 0

    def load_copy(i):
        if i == 4:
            return pltpu.make_async_copy(sketch_ref, sketch, load.at[4])
        part = pl.ds(256 * i, 256)
        return pltpu.make_async_copy(matrix_ref.at[part, :], matrix.at[part, :], load.at[i])

    for i in (4, 0, 1, 2, 3):
        load_copy(i).start()

    barrier = pltpu.get_barrier_semaphore()

    def greet(row, sample):
        pl.semaphore_signal(barrier, inc=1, device_id=(row, sample), device_id_type=MESH)

    def send(src, dst, sems, to):
        return pltpu.make_async_remote_copy(
            src_ref=src, dst_ref=dst, send_sem=sems[0], recv_sem=sems[1], device_id=to, device_id_type=MESH)

    greet(r, twin)
    greet(r, beside[0])
    greet(r, beside[1])
    greet(r, across[0])
    greet(r, across[1])

    @pl.when(odd)
    def _():
        greet(r - 1, s)

    @pl.when(jnp.logical_and(even, jnp.logical_not(helper)))
    def _():
        greet(jnp.where(level2, r - 1, r - 2), s)
        greet(jnp.where(level2, r + 1, r + 2), s)

    @pl.when(helper)
    def _():
        for z in range(1, 8):
            greet(r + z, s)

    @pl.when(level4)
    def _():
        greet(r - 8, s)

    @pl.when(root)
    def _():
        for y in range(1, 4):
            greet((r + 8 * y) % 32, s)

    again = listed(piv_ref[0, 2:3, :], 512)
    handed = [
        jnp.dot(listed(piv_ref[0, h:h + 1, :], 512), again[256 * h:256 * h + 256],
                preferred_element_type=jnp.float32).astype(jnp.bfloat16)
        for h in range(2)
    ]
    load_copy(4).wait()
    for i in range(4):
        load_copy(i).wait()
        product = jnp.dot(matrix[256 * i:256 * i + 256, :], sketch[...], preferred_element_type=jnp.float32)
        pt_ref[:, 256 * i:256 * i + 256] = product.T
    early[...] = pick_by(pt_ref[:, :512], handed[0]) + pick_by(pt_ref[:, 512:], handed[1])

    pl.semaphore_wait(barrier, 7 + jnp.where(level2, 1, 0) + jnp.where(helper, 1, 0))

    def swap_copy(h):
        return send(
            pt_ref.at[pl.ds(pl.multiple_of(HALF * (1 - c), 8), HALF), pl.ds(512 * h, 512)], swap.at[h],
            (swap_send.at[h], swap_recv.at[h]), (r, twin))

    def swap_early():
        return send(
            early.at[pl.ds(pl.multiple_of(HALF * (1 - c), 8), HALF), :], swap0,
            (swap_send.at[2], swap_recv.at[2]), (r, twin))

    swap_early().start()
    swap_copy(0).start()
    swap_copy(1).start()
    group = r // 8

    @pl.when(helper)
    def _():
        top = listed(node_ref[pl.ds(2 + group, 1), :], 512)
        for q in range(2):
            middle = jnp.dot(listed(node_ref[pl.ds(6 + 2 * group + q, 1), :], 512), top[256 * q:256 * q + 256],
                             preferred_element_type=jnp.float32).astype(jnp.bfloat16)
            for p in range(2):
                lower = listed(node_ref[pl.ds(14 + 4 * group + 2 * q + p, 1), :], 512)
                composed[512 * (2 * q + p):512 * (2 * q + p) + 512, :] = jnp.dot(
                    lower, middle[256 * p:256 * p + 256], preferred_element_type=jnp.float32).astype(jnp.bfloat16)

    def share(d, first=0, count=SHARE):
        return pl.ds(pl.multiple_of(SHARE * ((x + d) % 4) + first, 8), count)

    def pass_copy(h, way):
        return send(
            half_sum.at[h, share(2, PART * way, PART), :], passing.at[h, way],
            (pass_send.at[h, way], pass_recv.at[h, way]), (r, beside[way]))

    def part_copy(h, way):
        return send(
            half_sum.at[h, share((1, 3)[way]), :], parts.at[h, way],
            (part_send.at[h, way], part_recv.at[h, way]), (r, beside[way]))

    def pass_early(way):
        return send(
            sum0.at[share(2, PART * way, PART), :], passing0.at[way],
            (pass_send.at[2, way], pass_recv.at[2, way]), (r, beside[way]))

    def part_early(way):
        return send(
            sum0.at[share((1, 3)[way]), :], parts0.at[way],
            (part_send.at[2, way], part_recv.at[2, way]), (r, beside[way]))

    swap_early().wait_recv()
    sum0[...] = early[pl.ds(pl.multiple_of(HALF * c, 8), HALF), :] + swap0[...]
    for way in range(2):
        pass_early(way).start()
    def pass_main(h):
        swap_copy(h).wait_recv()
        half_sum[h] = pt_ref[pl.ds(pl.multiple_of(HALF * c, 8), HALF), 512 * h:512 * h + 512] + swap[h]
        for way in range(2):
            pass_copy(h, way).start()

    pass_main(0)
    for way in range(2):
        pass_early(way).wait_recv()
        sum0[share((1, 3)[way], PART * way, PART), :] += passing0[way]
        part_early(way).start()
    pass_main(1)
    for way in range(2):
        part_early(way).wait_recv()
    skeleton = sum0[share(0), :] + parts0[0] + parts0[1]

    def skeleton_copy():
        return send(below, climb_in.at[:, pl.ds(0, 256)], (tree_send.at[0], tree_recv.at[0]), (r + 1, s))

    def ring_copy():
        return send(
            below, ring_in.at[:, pl.ds(pl.multiple_of(256 * (r % 8), 128), 256)],
            (tree_send.at[2], ring_recv.at[r % 8]), (r - r % 8, s))

    below[...] = skeleton

    @pl.when(helper)
    def _():
        ring_in[:, :256] = skeleton

    @pl.when(jnp.logical_not(helper))
    def _():
        ring_copy().start()

    @pl.when(odd)
    def _():
        climb_in[:, 256:] = skeleton

    @pl.when(even)
    def _():
        skeleton_copy().start()

    for h in range(2):
        for way in range(2):
            pass_copy(h, way).wait_recv()
            mine = share((1, 3)[way], PART * way, PART)
            half_sum[h, mine, :] += passing[h, way]
            part_copy(h, way).start()

    def place(d, first=0, count=SHARE):
        return pl.ds(pl.multiple_of(HALF * c + SHARE * ((x + d) % 4) + first, 8), count)

    outs = (leaf_ref, stk_ref, up_ref)
    OFFSET = (1, 3)

    def direct_copy(n, way, part):
        if n == 0:
            src, dst = own.at[((x + OFFSET[way]) % 4) // 2], leaf_ref.at[place(0), :]
        else:
            first = PART * (way if part == 0 else 1 - way)
            src = (own_stk, climb_in)[n - 1].at[pl.ds(first, PART), :]
            dst = outs[n].at[place(0, first, PART), :]
        return send(src, dst, (direct_send.at[n, way, part], direct_recv.at[n, way, part]), (r, beside[way]))

    def relay_copy(n, way):
        back = OFFSET[1 - way]
        region = outs[n].at[place(back, PART * way, PART), :]
        return send(region, region, (relay_send.at[n, way], relay_recv.at[n, way]), (r, beside[way]))

    def cross_copy(way):
        region = up_ref.at[place(OFFSET[1 - way], PART * way, PART), :]
        return send(region, region, (cross_send.at[way], cross_recv.at[way]), (r, across[way]))

    def cross_arrived(way):
        region = up_ref.at[pl.ds(pl.multiple_of(HALF * (1 - c) + SHARE * ((x + 2) % 4) + PART * way, 8), PART), :]
        send(region, region, (cross_send.at[way], cross_recv.at[way]), (r, across[way])).wait_recv()

    first_of_pair = (x % 2) == 0
    mate = jnp.where(first_of_pair, beside[0], beside[1])

    def leaf_relay():
        region = leaf_ref.at[place(jnp.where(first_of_pair, 3, 1)), :]
        return send(region, region, (relay_send.at[0, 0], relay_recv.at[0, 0]), (r, mate))

    def pair_copy(n, d):
        region = outs[n].at[place(d), :]
        return send(region, region, (pair_send.at[n, d], pair_recv.at[n, d]), (r, twin))

    def spread(n):
        for part in range(1 if n == 0 else 2):
            for way in range(2):
                direct_copy(n, way, part).start()
        pair_copy(n, 0).start()

    def collect(n):
        for way in range(2):
            direct_copy(n, way, 0).wait_recv()
            if n > 0:
                relay_copy(n, way).start()
            if n == 2:
                cross_copy(way).start()
        if n == 0:
            leaf_relay().start()
        for way in range(2):
            if n > 0:
                direct_copy(n, way, 1).wait_recv()
            pair_copy(n, OFFSET[1 - way]).start()

    def finish(n):
        if n == 0:
            leaf_relay().wait_recv()
        else:
            for way in range(2):
                relay_copy(n, way).wait_recv()
        if n < 2:
            pair_copy(n, 2).start()

    node_row = jnp.where(odd, 14 + r // 2, 6 + r // 4)
    side = jnp.where(odd, (r // 2) % 2, (r // 4) % 2)
    where_to = pl.ds(pl.multiple_of(256 * side, 128), 256)

    def tree_copy(to, sem):
        return send(climb_out, climb_in.at[:, where_to], (tree_send.at[sem], tree_recv.at[side]), (to, s))

    mine_of_four = pl.ds(pl.multiple_of(256 * group, 128), 256)

    def column_copy(which):
        to = jnp.where(r == 0, 16, 0) if which == 0 else jnp.where(root, r + 8, 16)
        return send(
            height3, column_in.at[:, mine_of_four],
            (tree_send.at[1 + 2 * which], column_recv.at[group]), (to, s))

    def arrived(half):
        send(climb_out, climb_in.at[:, pl.ds(256 * half, 256)],
             (tree_send.at[1], tree_recv.at[half]), (r, twin)).wait_recv()

    def column_arrived(y):
        send(height3, column_in.at[:, pl.ds(pl.multiple_of(256 * y, 128), 256)],
             (tree_send.at[1], column_recv.at[y]), (r, twin)).wait_recv()

    def select():
        climb_out[...] = pick(climb_in[...], node_ref[pl.ds(node_row, 1), :])

    up_one = jnp.where(side == 0, r + 1, r - 1)
    up_two = jnp.where(side == 0, r + 2, r - 2)

    @pl.when(odd)
    def _():
        arrived(0)
        select()
        tree_copy(up_one, 1).start()

    for h in range(2):
        for way in range(2):
            part_copy(h, way).wait_recv()
        total = half_sum[h, share(0), :] + parts[h, 0] + parts[h, 1]
        own[h] = total
        own_stk[:, 256 * h:256 * h + 256] = pick(total, piv_ref[0, h:h + 1, :])
    stacked = own_stk[...]
    leaf_ref[place(0), :] = own[x // 2]
    stk_ref[place(0), :] = stacked

    spread(0)
    spread(1)

    @pl.when(level2)
    def _():
        arrived(0)
        arrived(1)
        select()
        tree_copy(up_two, 1).start()

    @pl.when(helper)
    def _():
        for z in range(1, 8):
            send(below, ring_in.at[:, pl.ds(256 * z, 256)],
                 (tree_send.at[2], ring_recv.at[z]), (r, twin)).wait_recv()
        found = pick_by(ring_in[...], composed[...])
        height3[...] = found
        column_in[:, mine_of_four] = found
        for which in range(2):
            column_copy(which).start()

    collect(0)
    collect(1)

    later = jnp.logical_or(odd, jnp.logical_or(level2, helper))

    @pl.when(jnp.logical_not(later))
    def _():
        finish(0)
        finish(1)

    @pl.when(level4)
    def _():
        column_arrived(group - 1)
        climb_in[...] = column_in[:, pl.ds(pl.multiple_of(512 * (group // 2), 128), 512)]

    @pl.when(root)
    def _():
        for y in range(1, 4):
            column_arrived((group + y) % 4)
        for j in range(2):
            climb_in[:, 256 * j:256 * j + 256] = pick(column_in[:, 512 * j:512 * j + 512], node_ref[j:j + 1, :])

    @pl.when((r % 8) == 4)
    def _():
        arrived(0)
        arrived(1)

    up_ref[place(0), :] = climb_in[...]
    spread(2)

    @pl.when(later)
    def _():
        finish(0)
        finish(1)

    collect(2)
    finish(2)

    swap_early().wait_send()
    for way in range(2):
        pass_early(way).wait_send()
        part_early(way).wait_send()
    for h in range(2):
        swap_copy(h).wait_send()
        for way in range(2):
            pass_copy(h, way).wait_send()
            part_copy(h, way).wait_send()

    @pl.when(even)
    def _():
        skeleton_copy().wait_send()

    @pl.when(odd)
    def _():
        tree_copy(up_one, 1).wait_send()

    @pl.when(level2)
    def _():
        tree_copy(up_two, 1).wait_send()

    @pl.when(helper)
    def _():
        for which in range(2):
            column_copy(which).wait_send()

    @pl.when(jnp.logical_not(helper))
    def _():
        ring_copy().wait_send()

    leaf_relay().wait_send()
    for n in range(3):
        for way in range(2):
            direct_copy(n, way, 0).wait_send()
            if n > 0:
                direct_copy(n, way, 1).wait_send()
                relay_copy(n, way).wait_send()
        for d in ((0, 1, 2, 3) if n < 2 else (0, 1, 3)):
            pair_copy(n, d).wait()
    for way in range(2):
        cross_copy(way).wait_send()
        cross_arrived(way)


def gathered(matrix, sketch, pivots, node_pivots):
    vmem = pl.BlockSpec(memory_space=pltpu.VMEM)
    f32 = jnp.float32
    dma = pltpu.SemaphoreType.DMA
    return pl.pallas_call(
        exchange,
        out_shape=[jax.ShapeDtypeStruct((384, 512), f32)] * 3,
        in_specs=[pl.BlockSpec(memory_space=pltpu.MemorySpace.HBM)] * 2 + [vmem] * 2, out_specs=[vmem] * 3,
        scratch_shapes=[
            pltpu.VMEM(matrix.shape, matrix.dtype), pltpu.VMEM(sketch.shape, sketch.dtype),
            pltpu.VMEM((384, 1024), f32), pltpu.VMEM((384, 256), f32), pltpu.VMEM((HALF, 256), f32), pltpu.VMEM((HALF, 256), f32),
            pltpu.VMEM((2, PART, 256), f32), pltpu.VMEM((2, SHARE, 256), f32), dma((5,)),
            pltpu.VMEM((2, HALF, 512), f32), pltpu.VMEM((2, HALF, 512), f32),
            pltpu.VMEM((2, 2, PART, 512), f32), pltpu.VMEM((2, 2, SHARE, 512), f32),
            pltpu.VMEM((2, SHARE, 512), f32), pltpu.VMEM((SHARE, 512), f32), pltpu.VMEM((SHARE, 256), f32),
            pltpu.VMEM((SHARE, 512), f32), pltpu.VMEM((SHARE, 256), f32),
            pltpu.VMEM((SHARE, 2048), f32), pltpu.VMEM((2048, 256), jnp.bfloat16),
            pltpu.VMEM((SHARE, 256), f32), pltpu.VMEM((SHARE, 1024), f32),
            dma((3,)), dma((3,)), dma((3, 2)), dma((3, 2)), dma((3, 2)), dma((3, 2)), dma((3, 2, 2)), dma((3, 2, 2)),
            dma((3, 2)), dma((3, 2)), dma((3, 4)), dma((3, 4)), dma((4,)), dma((2,)), dma((8,)), dma((4,)), dma((2,)), dma((2,)),
        ],
        compiler_params=pltpu.CompilerParams(collective_id=0, has_side_effects=True, vmem_limit_bytes=50 << 20),
        name="exchange",
    )(matrix, sketch, pivots, node_pivots)


def on_device(matrix_block, sketch_matrix, local_pivots, upper_pivots):
    return tuple(bases(*gathered(matrix_block, sketch_matrix, local_pivots, upper_pivots)))


def solution(mesh):
    in_specs = (P("rows", "samples"), P("samples", None), P("rows", None, None), P())
    out_specs = (P(("rows", "samples"), None), P("rows", None), P("rows", None))
    return jax.shard_map(
        on_device, mesh=mesh, in_specs=in_specs, out_specs=out_specs, check_vma=False
    )
```
